512 devices in a mesh: tile: 64 (over x, y, core), thick: 8 (over z).
Axes of the slice: x: 4, y: 8, z: 8, core: 2. Of those that a mesh axis runs over, the one named last changes fastest.
Arguments:
- velocity: float32 [3, 256, 128, 128], P(None, 'thick', 'tile'), may hold values from -6 to 6
- forcing: float32 [3, 256, 128, 128], P(None, 'thick', 'tile'), may hold values from -4 to 4
- viscosity: float32 [256, 128, 128], P('thick', 'tile'), may hold values from 0.1 to 1.6
- fibre: float32 [3, 256, 128, 128], P(None, 'thick', 'tile'), may hold values from -1.5 to 1.5
- inertia: float32 [256, 128, 128], P('thick', 'tile'), may hold values from 0.001 to 0.004
Outputs:
- update: float32 [3, 256, 128, 128], P(None, 'thick', 'tile')
- krylov_image: float32 [3, 256, 128, 128], P(None, 'thick', 'tile')
The draws below stay inside these ranges and needn't reach their ends.
All inputs are finite; a program needn't handle non-finite values.
Results may differ from the reference program's by a relative error of at most 0.0003.
Values sent between devices are 32-bit elements; how exact they have to be, the bound alone decides.
A program may use at most 64 MiB of HBM per device.

```python
import math
import jax
import jax.numpy as jnp
from jax import lax

NY = 128
NX = 128
NZ = 256


def draw_forcing(key, part):
    array_shape = (3, NZ, NX, NY)
    normal_part = jax.random.normal(key, array_shape, jnp.float32)
    return jnp.clip(normal_part, -4.0, 4.0)


def levels(key, shape, split, smallest, high):
    def one(position, parts):
        steps = jax.random.uniform(jax.random.fold_in(jax.random.fold_in(key, 6), position), (parts,), jnp.float32, smallest / len(split), high / len(split))
        return jnp.repeat(jnp.exp(steps), shape[position] // parts).reshape((-1,) + (1,) * (len(shape) - position - 1))

    factor_of = one(*split[0])
    for cut in split[1:]:
        factor_of = factor_of * one(*cut)
    return factor_of


def scatter_about(own_key, dims, scale, bound, cuts=(), kind=jnp.bfloat16):
    gain = levels(own_key, dims, cuts, -0.22, 0.18) if cuts else 1.0
    values = jax.random.normal(own_key, dims, jnp.float32) * scale * gain
    return jnp.minimum(jnp.maximum(values, -bound), bound).astype(kind)


def setup_inputs(seed: int = 0) -> dict:
    arg_keys = jax.random.split(jax.random.key(seed), 6)
    velocity = scatter_about(arg_keys[0], (3, NZ, NX, NY), 1.0, 6.0, ((1, 8), (2, 64)), jnp.float32)
    forcing = draw_forcing(jax.random.fold_in(arg_keys[5], 71), 0)
    viscosity = jnp.clip(jnp.exp(math.log(1.6) - 2.7725887 * jax.random.uniform(arg_keys[2], (NZ, NX, NY), jnp.float32) ** levels(arg_keys[2], (NZ, NX, NY), ((0, 8), (1, 64)), -0.2, 0.2)), 0.1, 1.6)
    fibre = scatter_about(arg_keys[3], (3, NZ, NX, NY), 0.5, 1.5, ((1, 8), (2, 64)), jnp.float32)
    inertia = jnp.clip(jnp.exp(math.log(0.004) - 1.3862944 * jax.random.uniform(arg_keys[4], (NZ, NX, NY), jnp.float32) ** levels(arg_keys[4], (NZ, NX, NY), ((0, 8), (1, 64)), -0.2, 0.2)), 0.001, 0.004)
    return {"velocity": velocity, "forcing": forcing, "viscosity": viscosity, "fibre": fibre, "inertia": inertia}


stencil_weights = {1: 1.0 / 3.0, 2: 1.0 / 6.0, 3: 1.0 / 12.0}


def lane_shift(values, offset):
    if offset == 0:
        return values
    zero_edge = jnp.zeros_like(values[..., :1])
    if offset > 0:
        return jnp.concatenate([values[..., 1:], zero_edge], axis=-1)
    return jnp.concatenate([zero_edge, values[..., :-1]], axis=-1)


def apply_stencil(field_pad, visc_pad):
    depth_cells = field_pad.shape[1] - 2
    span_cells = field_pad.shape[2] - 2
    centre = field_pad[:, 1:depth_cells + 1, 1:span_cells + 1]
    visc_centre = visc_pad[1:depth_cells + 1, 1:span_cells + 1]
    summed = jnp.zeros_like(centre)
    for step_z in (-1, 0, 1):
        for step_x in (-1, 0, 1):
            for step_y in (-1, 0, 1):
                distance = abs(step_z) + abs(step_x) + abs(step_y)
                if distance == 0:
                    continue
                neighbour = lane_shift(field_pad[:, 1 + step_z:depth_cells + 1 + step_z, 1 + step_x:span_cells + 1 + step_x], step_y)
                visc_other = lane_shift(visc_pad[1 + step_z:depth_cells + 1 + step_z, 1 + step_x:span_cells + 1 + step_x], step_y)
                summed = summed + (0.5 * stencil_weights[distance]) * (visc_centre + visc_other) * (centre - neighbour)
    return summed


def identity_block(rank_count):
    return jnp.eye(3, dtype=jnp.float32).reshape((3, 3) + (1,) * (rank_count - 2))


def face_blocks(visc_low, visc_high, fibre_low):
    face_visc = 0.5 * (visc_low + visc_high)
    matrix_rows = []
    for row_index in range(3):
        entries = []
        for col_index in range(3):
            product_term = fibre_low[row_index] * fibre_low[col_index]
            if row_index == col_index:
                product_term = product_term + 1.0
            entries.append(face_visc * product_term)
        matrix_rows.append(jnp.stack(entries))
    return jnp.stack(matrix_rows)


def line_blocks(visc_rows, fibre_rows, viscosity, inertia, keep_low, keep_high):
    face_mats = face_blocks(visc_rows[:-1], visc_rows[1:], fibre_rows[:, :-1])
    below_face = face_mats[:, :, :-1]
    above_face = face_mats[:, :, 1:]
    main_diagonal = below_face + above_face + identity_block(face_mats.ndim) * (inertia * viscosity)
    return -below_face * keep_low, main_diagonal, -above_face * keep_high


def block_product(left_blocks, right_blocks):
    result = left_blocks[:, 0][:, None] * right_blocks[0][None]
    for inner_index in range(1, left_blocks.shape[1]):
        result = result + left_blocks[:, inner_index][:, None] * right_blocks[inner_index][None]
    return result


def block_inverse(matrix):
    size_n = matrix.shape[0]
    working = [[matrix[row_index, col_index] for col_index in range(size_n)] for row_index in range(size_n)]
    unit_entry = jnp.ones_like(matrix[0, 0])
    zero_entry = jnp.zeros_like(matrix[0, 0])
    result = [[unit_entry if row_index == col_index else zero_entry for col_index in range(size_n)] for row_index in range(size_n)]
    for pivot_index in range(size_n):
        reciprocal = 1.0 / working[pivot_index][pivot_index]
        working[pivot_index] = [element * reciprocal for element in working[pivot_index]]
        result[pivot_index] = [element * reciprocal for element in result[pivot_index]]
        for row_index in range(size_n):
            if row_index != pivot_index:
                factor = working[row_index][pivot_index]
                working[row_index] = [working[row_index][col_index] - factor * working[pivot_index][col_index] for col_index in range(size_n)]
                result[row_index] = [result[row_index][col_index] - factor * result[pivot_index][col_index] for col_index in range(size_n)]
    return jnp.stack([jnp.stack(row_list) for row_list in result])


def move_rows(values, offset, fill_value):
    row_count = min(abs(offset), values.shape[2])
    pad_block = jnp.broadcast_to(fill_value, values.shape[:2] + (row_count,) + values.shape[3:]).astype(values.dtype)
    if offset > 0:
        return jnp.concatenate([pad_block, values[:, :, :values.shape[2] - row_count]], axis=2)
    return jnp.concatenate([values[:, :, row_count:], pad_block], axis=2)


def parallel_cyclic_level(band_lower, main_diagonal, band_upper, source_terms, rows_downward, rows_upward):
    alpha_left = -block_product(band_lower, block_inverse(rows_downward[1]))
    gamma_right = -block_product(band_upper, block_inverse(rows_upward[1]))
    new_lower = block_product(alpha_left, rows_downward[0])
    new_upper = block_product(gamma_right, rows_upward[2])
    new_diag = main_diagonal + block_product(alpha_left, rows_downward[2]) + block_product(gamma_right, rows_upward[0])
    new_source = source_terms + block_product(alpha_left, rows_downward[3]) + block_product(gamma_right, rows_upward[3])
    return new_lower, new_diag, new_upper, new_source


def solve_lines(band_lower, main_diagonal, band_upper, source_terms):
    row_total = main_diagonal.shape[2]
    eye_fill = identity_block(main_diagonal.ndim)
    zero_fill = jnp.zeros((), main_diagonal.dtype)
    offset = 1
    while offset < row_total:
        rows_downward = (move_rows(band_lower, offset, zero_fill), move_rows(main_diagonal, offset, eye_fill), move_rows(band_upper, offset, zero_fill), move_rows(source_terms, offset, zero_fill))
        rows_upward = (move_rows(band_lower, -offset, zero_fill), move_rows(main_diagonal, -offset, eye_fill), move_rows(band_upper, -offset, zero_fill), move_rows(source_terms, -offset, zero_fill))
        band_lower, main_diagonal, band_upper, source_terms = parallel_cyclic_level(band_lower, main_diagonal, band_upper, source_terms, rows_downward, rows_upward)
        offset = offset * 2
    return block_product(block_inverse(main_diagonal), source_terms)


def reference(velocity, forcing, viscosity, fibre, inertia):
    vel_pad = jnp.pad(velocity, ((0, 0), (1, 1), (1, 1), (0, 0)))
    visc_pad = jnp.pad(viscosity, ((1, 1), (1, 1), (0, 0)))
    residual = forcing - apply_stencil(vel_pad, visc_pad)
    total_rows = viscosity.shape[0]
    row_ids = jnp.arange(total_rows)
    keep_low = (row_ids != 0).astype(jnp.float32)[:, None]
    keep_high = (row_ids != total_rows - 1).astype(jnp.float32)[:, None]
    visc_rows = jnp.moveaxis(jnp.pad(viscosity, ((1, 1), (0, 0), (0, 0))), 1, 0)
    fibre_rows = jnp.moveaxis(jnp.pad(fibre, ((0, 0), (1, 1), (0, 0), (0, 0))), 2, 0)
    visc_cells = jnp.moveaxis(viscosity, 1, 0)
    inertia_cells = jnp.moveaxis(inertia, 1, 0)
    source_cells = jnp.moveaxis(residual, 2, 0)

    def one_slab(slab_items):
        v_rows, f_rows, v_cells, i_cells, s_cells = slab_items
        band_lower, main_diagonal, band_upper = line_blocks(v_rows, f_rows, v_cells, i_cells, keep_low, keep_high)
        return solve_lines(band_lower, main_diagonal, band_upper, s_cells[:, None])[:, 0]

    solved = lax.map(one_slab, (visc_rows, fibre_rows, visc_cells, inertia_cells, source_cells))
    update = jnp.moveaxis(solved, 0, 2)
    krylov_image = apply_stencil(jnp.pad(update, ((0, 0), (1, 1), (1, 1), (0, 0))), visc_pad)
    return update, krylov_image
```

```python
import functools

import jax
import jax.numpy as jnp
from jax import lax
from jax.experimental import pallas as pl
from jax.experimental.pallas import tpu as pltpu
from jax.sharding import PartitionSpec as P

MESH = pl.DeviceIdType.MESH
SLICES = 8
SYM = ((0, 1, 2), (1, 3, 4), (2, 4, 5))
TILE = (8, 128)


def roll_rows(values, shift):
    return values if shift % 8 == 0 else pltpu.roll(values, shift % 8, 0)


def row_ids():
    return lax.broadcasted_iota(jnp.int32, TILE, 0)


def load_slices(ref, lead=()):
    def one(v):
        halves = [ref[lead + (pl.ds(2 * v + x, 4, stride=16), slice(None))] for x in (0, 1)]
        return jnp.concatenate(halves, axis=0)

    return [one(v) for v in range(SLICES)]


def store_slices(ref, lead, slices):
    for v in range(SLICES):
        for x in (0, 1):
            ref[lead + (pl.ds(2 * v + x, 4, stride=16), slice(None))] = slices[v][4 * x : 4 * x + 4]


def pack_rows(fields, pos):
    rows = row_ids() % 4
    packed = roll_rows(fields[0], -pos)
    for j in range(1, len(fields)):
        packed = jnp.where(rows == j, roll_rows(fields[j], j - pos), packed)
    return packed


def pack_sides(left_ref, right_ref, fields):
    low = row_ids() < 4
    for j, slices in enumerate(fields):
        for m in range(4):
            first, second = slices[2 * m], slices[2 * m + 1]
            left_ref[4 * j + m] = jnp.where(low, first, roll_rows(second, 4))
            right_ref[4 * j + m] = jnp.where(low, roll_rows(first, 4), second)


def neighbours(tiles, groups):
    t, k = lax.axis_index("tile"), lax.axis_index("thick")
    left, right = lax.rem(t + tiles - 1, tiles), lax.rem(t + 1, tiles)
    down, up = lax.rem(k + groups - 1, groups), lax.rem(k + 1, groups)
    return [
        (left, k), (right, k), (t, up), (t, down),
        (right, up), (left, up), (right, down), (left, down),
    ]


def greet(targets):
    barrier = pltpu.get_barrier_semaphore()
    for target in targets:
        pl.semaphore_signal(barrier, inc=1, device_id=target, device_id_type=MESH)
    pl.semaphore_wait(barrier, len(targets))


def exchange(targets, sent, landed, send_sems, recv_sems):
    copies = [
        pltpu.make_async_remote_copy(
            src_ref=src, dst_ref=dst, send_sem=send_sems.at[i], recv_sem=recv_sems.at[i],
            device_id=target, device_id_type=MESH,
        )
        for i, (target, src, dst) in enumerate(zip(targets, sent, landed))
    ]
    for copy in copies:
        copy.start()
    for copy in copies:
        copy.wait()


def halo_out(tx_left, tx_right, tx_top, tx_bot):
    corner = tx_top.at[pl.ds(0, 1)]
    return [tx_left, tx_right, tx_top, tx_bot, corner, corner, tx_bot, tx_bot]


def halo_in(rx_left, rx_right, rx_below, rx_rest):
    rest = [rx_rest.at[pl.ds(i, 1)] for i in range(5)]
    return [rx_right, rx_left, rx_below] + rest


def first_halo_kernel(
    tiles, groups, vel, visc, fibre, rx_left, rx_right, rx_below, rx_rest,
    tx_left, tx_right, tx_top, tx_bot, send_sems, recv_sems,
):
    targets = neighbours(tiles, groups)
    fields = [load_slices(vel, (c,)) for c in range(3)] + [load_slices(visc)]
    pack_sides(tx_left, tx_right, fields)
    tx_bot[0] = pack_rows([f[0] for f in fields], 0)
    tx_top[0] = pack_rows([f[7] for f in fields], 3)
    tx_top[1] = pack_rows([load_slices(fibre, (c,))[7] for c in range(3)], 3)
    greet(targets)
    exchange(
        targets, halo_out(tx_left, tx_right, tx_top, tx_bot),
        halo_in(rx_left, rx_right, rx_below, rx_rest), send_sems, recv_sems,
    )


def second_halo_kernel(
    tiles, groups, update, rx_left, rx_right, rx_below, rx_rest,
    tx_left, tx_right, tx_top, tx_bot, send_sems, recv_sems,
):
    targets = neighbours(tiles, groups)
    fields = [load_slices(update, (c,)) for c in range(3)]
    pack_sides(tx_left, tx_right, fields)
    tx_bot[0] = pack_rows([f[0] for f in fields], 0)
    tx_top[0] = pack_rows([f[7] for f in fields], 3)
    greet(targets)
    exchange(
        targets, halo_out(tx_left, tx_right, tx_top, tx_bot),
        halo_in(rx_left, rx_right, rx_below, rx_rest), send_sems, recv_sems,
    )


def gather_kernel(groups, own, gathered, send_sems, recv_sems):
    t, k = lax.axis_index("tile"), lax.axis_index("thick")
    targets = [(t, lax.rem(k + d, groups)) for d in range(1, groups)]
    greet(targets)
    copies = [
        pltpu.make_async_remote_copy(
            src_ref=own, dst_ref=gathered.at[k], send_sem=send_sems.at[i], recv_sem=recv_sems.at[i],
            device_id=target, device_id_type=MESH,
        )
        for i, target in enumerate(targets)
    ]
    for copy in copies:
        copy.start()
    gathered[k] = own[...]
    for copy in copies:
        copy.wait()


def edges(tiles, groups):
    t, k = lax.axis_index("tile"), lax.axis_index("thick")
    rows = row_ids()
    low = rows < 4
    side_ok = jnp.logical_or(
        jnp.logical_and(low, t > 0), jnp.logical_and(jnp.logical_not(low), t < tiles - 1)
    )
    return rows, low, side_ok, k > 0, k < groups - 1


def below_slice(slices, packed, j, has_below, rows):
    inside = roll_rows(slices[7], 1)
    return jnp.where(rows % 4 == 0, jnp.where(has_below, roll_rows(packed, -j), 0.0), inside)


def above_slice(slices, packed, j, has_above, rows):
    inside = roll_rows(slices[0], -1)
    return jnp.where(rows % 4 == 3, jnp.where(has_above, roll_rows(packed, 3 - j), 0.0), inside)


def extended(slices, j, rx_left, rx_right, rx_below, rx_rest, place):
    rows, low, side_ok, has_below, has_above = place
    sides = []
    for m in range(4):
        left, right = rx_left[4 * j + m], rx_right[4 * j + m]
        sides.append(jnp.where(side_ok, jnp.where(low, left, roll_rows(right, 4)), 0.0))
        sides.append(jnp.where(side_ok, jnp.where(low, roll_rows(left, 4), right), 0.0))
    centre = (
        [below_slice(slices, rx_below[0], j, has_below, rows)]
        + slices
        + [above_slice(slices, rx_rest[0], j, has_above, rows)]
    )
    below = roll_rows(jnp.where(low, rx_rest[2], rx_rest[1]), 4 - j)
    above = roll_rows(jnp.where(low, rx_rest[4], rx_rest[3]), 7 - j)
    below = jnp.where(jnp.logical_and(side_ok, has_below), below, 0.0)
    above = jnp.where(jnp.logical_and(side_ok, has_above), above, 0.0)
    sides = (
        [jnp.where(rows % 4 == 0, below, roll_rows(sides[7], 1))]
        + sides
        + [jnp.where(rows % 4 == 3, above, roll_rows(sides[0], -1))]
    )
    return centre, sides


def smooth(centre, sides):
    lanes = lax.broadcasted_iota(jnp.int32, TILE, 1)
    across = [c + 0.5 * (roll_rows(c, 4) + s) for c, s in zip(centre, sides)]
    out = []
    for v in range(SLICES):
        z = across[v + 1] + 0.5 * (across[v] + across[v + 2])
        up = jnp.where(lanes < 127, pltpu.roll(z, 127, 1), 0.0)
        down = jnp.where(lanes > 0, pltpu.roll(z, 1, 1), 0.0)
        out.append(z + 0.5 * (up + down))
    return out


def stencil(field, visc, weight):
    centre, sides = field
    visc_centre, visc_sides = visc
    flat = smooth(centre, sides)
    scaled = smooth(
        [a * b for a, b in zip(visc_centre, centre)], [a * b for a, b in zip(visc_sides, sides)]
    )
    return [
        (1.0 / 3.0) * (centre[v + 1] * weight[v] - visc_centre[v + 1] * flat[v] - scaled[v])
        for v in range(SLICES)
    ]


def stencil_weight(visc):
    flat = smooth(*visc)
    return [8.0 * visc[0][v + 1] + flat[v] for v in range(SLICES)]


def sym_inverse(d):
    a, b, c, e, f, g = d
    c00, c01, c02 = e * g - f * f, c * f - b * g, b * f - c * e
    r = 1.0 / (a * c00 + b * c01 + c * c02)
    return [r * q for q in (c00, c01, c02, a * g - c * c, b * c - a * f, a * e - b * b)]


def dot3(xs, ys):
    return xs[0] * ys[0] + xs[1] * ys[1] + xs[2] * ys[2]


def mat_vec(m, x):
    return [dot3(m[i], x) for i in range(3)]


def mat_mat(m, n):
    return [[dot3(m[i], [n[0][j], n[1][j], n[2][j]]) for j in range(3)] for i in range(3)]


def sym_product(m, n):
    return [dot3(m[i], [n[0][j], n[1][j], n[2][j]]) for i in range(3) for j in range(i, 3)]


def transposed(m):
    return [[m[j][i] for j in range(3)] for i in range(3)]


def full(d):
    return [[d[SYM[i][j]] for j in range(3)] for i in range(3)]


def eliminate(diag, source, to_prev, next_to):
    inv = full(sym_inverse(diag))
    pm = mat_mat(inv, to_prev)
    qm = mat_mat(inv, transposed(next_to))
    y = mat_vec(inv, source)
    prev_t = transposed(to_prev)
    return (
        (y, pm, qm),
        (sym_product(prev_t, pm), mat_vec(prev_t, y)),
        (sym_product(next_to, qm), mat_vec(next_to, y), mat_mat(next_to, pm)),
    )


def back(solved, x_prev, x_next):
    y, pm, qm = solved
    return [y[i] + dot3(pm[i], x_prev) + dot3(qm[i], x_next) for i in range(3)]


def minus(a, b):
    return [x - y for x, y in zip(a, b)]


def plus(a, b):
    return [x + y for x, y in zip(a, b)]


def select(mask, a, b):
    return [jnp.where(mask, x, y) for x, y in zip(a, b)]


def keep(mask, a):
    return [jnp.where(mask, x, 0.0) for x in a]


def moved(a, shift):
    return [roll_rows(x, shift) for x in a]


def moved_mat(m, shift):
    return [moved(r, shift) for r in m]


def reduce_rows(diag, source, link, pos):
    even = pos % 2 == 0
    done4, to_p, to_n = eliminate(diag, source, link, moved_mat(link, -1))
    base_d, base_s = keep(pos == 0, to_p[0]), keep(pos == 0, to_p[1])
    one = pos == 1
    diag = minus(diag, plus(moved(to_n[0], 1), keep(one, moved(to_p[0], -1))))
    source = plus(source, plus(moved(to_n[1], 1), keep(one, moved(to_p[1], -1))))
    link = moved_mat(to_n[2], 1)
    done5, to_p, to_n = eliminate(diag, source, link, moved_mat(link, -2))
    zero = pos == 0
    base_d = plus(base_d, keep(zero, moved(to_p[0], -1)))
    base_s = plus(base_s, keep(zero, moved(to_p[1], -1)))
    diag = minus(diag, moved(to_n[0], 2))
    source = plus(source, moved(to_n[1], 2))
    link = moved_mat(to_n[2], 2)
    return done4, done5, base_d, base_s, diag, source, link


def expand_rows(done4, done5, x_base, x_last, pos):
    x_one = back(done5, moved(x_base, 1), moved(x_last, -2))
    kept = select(pos == 1, x_one, x_last)
    x_even = back(done4, select(pos == 0, x_base, moved(kept, 1)), moved(kept, -1))
    return select(pos % 2 == 0, x_even, kept)


def flat_done(done):
    y, pm, qm = done
    return list(y) + [e for r in pm for e in r] + [e for r in qm for e in r]


def unflat_done(ref, i):
    e = [ref[i, j] for j in range(21)]
    return e[0:3], [e[3:6], e[6:9], e[9:12]], [e[12:15], e[15:18], e[18:21]]


def local_kernel(
    tiles, groups, vel, forcing, visc, fibre, inertia, rx_left, rx_right, rx_below, rx_rest,
    reduced, stash,
):
    place = edges(tiles, groups)
    rows, low, side_ok, has_below, has_above = place
    pos = rows % 4
    halo = (rx_left, rx_right, rx_below, rx_rest, place)
    visc_ext = extended(load_slices(visc), 3, *halo)
    weight = stencil_weight(visc_ext)
    source = [[] for _ in range(SLICES)]
    for c in range(3):
        image = stencil(extended(load_slices(vel, (c,)), c, *halo), visc_ext, weight)
        force = load_slices(forcing, (c,))
        for v in range(SLICES):
            source[v].append(force[v] - image[v])
    fib = [load_slices(fibre, (c,)) for c in range(3)]
    fib = [[below_slice(fib[c], rx_below[1], c, has_below, rows)] + fib[c] for c in range(3)]
    centre = visc_ext[0]
    face = []
    for v in range(SLICES + 1):
        mu = 0.5 * (centre[v] + centre[v + 1])
        f = [fib[c][v] for c in range(3)]
        g = [mu * q for q in f]
        face.append(
            [mu + g[0] * f[0], g[0] * f[1], g[0] * f[2], mu + g[1] * f[1], g[1] * f[2], mu + g[2] * f[2]]
        )
    mass = load_slices(inertia)
    diag, link = [], []
    for v in range(SLICES):
        d = plus(face[v], face[v + 1])
        m = mass[v] * centre[v + 1]
        for i in (0, 3, 5):
            d[i] = d[i] + m
        diag.append(d)
        link.append(full(face[v]))
    joined = jnp.logical_or(pos > 0, has_below)
    link[0] = [keep(joined, r) for r in link[0]]
    done = []
    low_d, low_s = None, None
    for step in (1, 2, 4):
        for e in range(step - 1, SLICES - 1, 2 * step):
            n, p = e + step, e - step
            solved, to_p, to_n = eliminate(diag[e], source[e], link[e], link[n])
            done.append(solved)
            diag[n], source[n], link[n] = minus(diag[n], to_n[0]), plus(source[n], to_n[1]), to_n[2]
            if p >= 0:
                diag[p], source[p] = minus(diag[p], to_p[0]), plus(source[p], to_p[1])
            elif low_d is None:
                low_d, low_s = to_p
            else:
                low_d, low_s = plus(low_d, to_p[0]), plus(low_s, to_p[1])
    inner = pos < 3
    d7 = minus(diag[7], keep(inner, moved(low_d, -1)))
    s7 = plus(source[7], keep(inner, moved(low_s, -1)))
    done4, done5, base_d, base_s, last_d, last_s, last_l = reduce_rows(d7, s7, link[7], pos)
    done += [done4, done5]
    base_d, base_s = plus(base_d, low_d), plus(base_s, low_s)
    out = moved(base_d, 3) + moved(base_s, 3) + last_d + last_s + [e for r in last_l for e in r]
    for i in range(7):
        reduced[i] = pack_rows(out[4 * i : 4 * i + 4], 3)
    for i, solved in enumerate(done):
        for j, e in enumerate(flat_done(solved)):
            stash[i, j] = e


def solve_kernel(groups, gathered, stash, update):
    k = lax.axis_index("thick")
    pos = row_ids() % 4

    def field(f, h):
        value = None
        for s in range(4):
            part = roll_rows(gathered[2 * s + h, f // 4], s - f % 4)
            value = part if value is None else jnp.where(pos == s, part, value)
        return value

    def fields(lo, hi, h):
        return [field(f, h) for f in range(lo, hi)]

    def link_of(h):
        e = fields(18, 27, h)
        return [e[0:3], e[3:6], e[6:9]]

    inner = pos < 3
    d0 = minus(fields(9, 15, 0), fields(0, 6, 1))
    s0 = plus(fields(15, 18, 0), fields(6, 9, 1))
    d1 = minus(fields(9, 15, 1), keep(inner, moved(fields(0, 6, 0), -1)))
    s1 = plus(fields(15, 18, 1), keep(inner, moved(fields(6, 9, 0), -1)))
    done_h, to_p, to_n = eliminate(d0, s0, link_of(0), link_of(1))
    d1 = minus(minus(d1, to_n[0]), keep(inner, moved(to_p[0], -1)))
    s1 = plus(plus(s1, to_n[1]), keep(inner, moved(to_p[1], -1)))
    done4, done5, _, _, last_d, last_s, _ = reduce_rows(d1, s1, to_n[2], pos)
    x_last = mat_vec(full(sym_inverse(last_d)), last_s)
    nothing = [jnp.zeros(TILE, jnp.float32)] * 3
    x1 = expand_rows(done4, done5, nothing, x_last, pos)
    x0 = back(done_h, keep(pos > 0, moved(x1, 1)), x1)
    own, base = nothing, nothing
    for g in range(groups):
        x = (x0, x1)[g % 2]
        own = select(k == g, moved(x, 3 - g // 2), own)
        base = select(k == g + 1, moved(x, -(g // 2)), base)
    done = [unflat_done(stash, i) for i in range(9)]
    x = [None] * SLICES
    x[7] = expand_rows(done[7], done[8], base, own, pos)
    under = select(pos == 0, base, moved(x[7], 1))
    x[3] = back(done[6], under, x[7])
    x[1] = back(done[4], under, x[3])
    x[5] = back(done[5], x[3], x[7])
    x[0] = back(done[0], under, x[1])
    for i, v in enumerate((2, 4, 6)):
        x[v] = back(done[1 + i], x[v - 1], x[v + 1])
    for c in range(3):
        store_slices(update, (c,), [x[v][c] for v in range(SLICES)])


def image_kernel(
    tiles, groups, update, visc, v_left, v_right, v_below, v_rest,
    rx_left, rx_right, rx_below, rx_rest, image,
):
    place = edges(tiles, groups)
    visc_ext = extended(load_slices(visc), 3, v_left, v_right, v_below, v_rest, place)
    weight = stencil_weight(visc_ext)
    for c in range(3):
        field = extended(
            load_slices(update, (c,)), c, rx_left, rx_right, rx_below, rx_rest, place
        )
        store_slices(image, (c,), stencil(field, visc_ext, weight))


def tiles_of(count):
    return jax.ShapeDtypeStruct((count,) + TILE, jnp.float32)


def call(kernel, name, out_shape, scratch=(), collective_id=None):
    vmem = pl.BlockSpec(memory_space=pltpu.VMEM)

    def run(*operands):
        return pl.pallas_call(
            kernel,
            out_shape=out_shape,
            in_specs=[vmem] * len(operands),
            out_specs=jax.tree.map(lambda _: vmem, out_shape),
            scratch_shapes=list(scratch),
            compiler_params=pltpu.CompilerParams(
                collective_id=collective_id, has_side_effects=collective_id is not None,
                vmem_limit_bytes=16 * 1024 * 1024,
            ),
            name=name,
        )(*operands)

    return run


def halo_call(kernel, name, fields, top, collective_id):
    sides = 4 * fields
    buffers = [pltpu.VMEM((n,) + TILE, jnp.float32) for n in (sides, sides, top, 1)]
    sems = [pltpu.SemaphoreType.DMA((8,)), pltpu.SemaphoreType.DMA((8,))]
    out = [tiles_of(n) for n in (sides, sides, top, 5)]
    return call(kernel, name, out, buffers + sems, collective_id)


def per_device(tiles, groups, velocity, forcing, viscosity, fibre, inertia):
    vel, force, fib = (a.reshape(3, 64, 128) for a in (velocity, forcing, fibre))
    visc, mass = viscosity.reshape(64, 128), inertia.reshape(64, 128)
    bind = functools.partial
    halo = halo_call(bind(first_halo_kernel, tiles, groups), "halo_a", 4, 2, 0)(vel, visc, fib)
    stash_shape = jax.ShapeDtypeStruct((9, 21) + TILE, jnp.float32)
    reduced, stash = call(bind(local_kernel, tiles, groups), "local", [tiles_of(7), stash_shape])(
        vel, force, visc, fib, mass, *halo
    )
    sems = [pltpu.SemaphoreType.DMA((groups - 1,)), pltpu.SemaphoreType.DMA((groups - 1,))]
    gathered_shape = jax.ShapeDtypeStruct((groups, 7) + TILE, jnp.float32)
    gathered = call(bind(gather_kernel, groups), "gather", gathered_shape, sems, 1)(reduced)
    block = jax.ShapeDtypeStruct((3, 64, 128), jnp.float32)
    update = call(bind(solve_kernel, groups), "solve", block)(gathered, stash)
    halo2 = halo_call(bind(second_halo_kernel, tiles, groups), "halo_b", 3, 1, 2)(update)
    image = call(bind(image_kernel, tiles, groups), "image", block)(update, visc, *halo, *halo2)
    return update.reshape(velocity.shape), image.reshape(velocity.shape)


def solution(mesh):
    wide, flat = P(None, "thick", "tile", None), P("thick", "tile", None)
    return jax.shard_map(
        functools.partial(per_device, mesh.shape["tile"], mesh.shape["thick"]),
        mesh=mesh,
        in_specs=(wide, wide, flat, wide, flat),
        out_specs=(wide, wide),
        check_vma=False,
    )
```

```python
import functools

import jax
import jax.numpy as jnp
from jax import lax
from jax.experimental import pallas as pl
from jax.experimental.pallas import tpu as pltpu
from jax.sharding import PartitionSpec as P

MESH = pl.DeviceIdType.MESH
SLICES = 8
SYM = ((0, 1, 2), (1, 3, 4), (2, 4, 5))
TILE = (8, 128)


def roll_rows(values, shift):
    return values if shift % 8 == 0 else pltpu.roll(values, shift % 8, 0)


def row_ids():
    return lax.broadcasted_iota(jnp.int32, TILE, 0)


def load_slices(ref, lead=()):
    def one(v):
        halves = [ref[lead + (pl.ds(2 * v + x, 4, stride=16), slice(None))] for x in (0, 1)]
        return jnp.concatenate(halves, axis=0)

    return [one(v) for v in range(SLICES)]


def store_slices(ref, lead, slices):
    for v in range(SLICES):
        for x in (0, 1):
            ref[lead + (pl.ds(2 * v + x, 4, stride=16), slice(None))] = slices[v][4 * x : 4 * x + 4]


def pack_rows(fields, pos):
    rows = row_ids() % 4
    packed = roll_rows(fields[0], -pos)
    for j in range(1, len(fields)):
        packed = jnp.where(rows == j, roll_rows(fields[j], j - pos), packed)
    return packed


def pack_sides(left_ref, right_ref, fields):
    low = row_ids() < 4
    for j, slices in enumerate(fields):
        for m in range(4):
            first, second = slices[2 * m], slices[2 * m + 1]
            left_ref[4 * j + m] = jnp.where(low, first, roll_rows(second, 4))
            right_ref[4 * j + m] = jnp.where(low, roll_rows(first, 4), second)


def greet(targets):
    barrier = pltpu.get_barrier_semaphore()
    count = 0
    for target, there in targets:
        if there is None:
            pl.semaphore_signal(barrier, inc=1, device_id=target, device_id_type=MESH)
            count = count + 1
        else:

            @pl.when(there)
            def _():
                pl.semaphore_signal(barrier, inc=1, device_id=target, device_id_type=MESH)

            count = count + there.astype(jnp.int32)
    return lambda: pl.semaphore_wait(barrier, count)


def remote(src, dst, send_sem, recv_sem, target):
    return pltpu.make_async_remote_copy(
        src_ref=src, dst_ref=dst, send_sem=send_sem, recv_sem=recv_sem,
        device_id=target, device_id_type=MESH,
    )


def when(there, action):
    pl.when(there)(lambda: action())


def edges(tiles, groups):
    t, k = lax.axis_index("tile"), lax.axis_index("thick")
    rows = row_ids()
    low = rows < 4
    side_ok = jnp.logical_or(
        jnp.logical_and(low, t > 0), jnp.logical_and(jnp.logical_not(low), t < tiles - 1)
    )
    return rows, low, side_ok, k > 0, k < groups - 1


def below_slice(slices, packed, j, has_below, rows):
    inside = roll_rows(slices[7], 1)
    return jnp.where(rows % 4 == 0, jnp.where(has_below, roll_rows(packed, -j), 0.0), inside)


def above_slice(slices, packed, j, has_above, rows):
    inside = roll_rows(slices[0], -1)
    return jnp.where(rows % 4 == 3, jnp.where(has_above, roll_rows(packed, 3 - j), 0.0), inside)


def extended(slices, j, rx_left, rx_right, rx_below, rx_rest, place):
    rows, low, side_ok, has_below, has_above = place
    sides = []
    for m in range(4):
        left, right = rx_left[4 * j + m], rx_right[4 * j + m]
        sides.append(jnp.where(side_ok, jnp.where(low, left, roll_rows(right, 4)), 0.0))
        sides.append(jnp.where(side_ok, jnp.where(low, roll_rows(left, 4), right), 0.0))
    centre = (
        [below_slice(slices, rx_below[0], j, has_below, rows)]
        + slices
        + [above_slice(slices, rx_rest[0], j, has_above, rows)]
    )
    below = roll_rows(jnp.where(low, rx_rest[2], rx_rest[1]), 4 - j)
    above = roll_rows(jnp.where(low, rx_rest[4], rx_rest[3]), 7 - j)
    below = jnp.where(jnp.logical_and(side_ok, has_below), below, 0.0)
    above = jnp.where(jnp.logical_and(side_ok, has_above), above, 0.0)
    sides = (
        [jnp.where(rows % 4 == 0, below, roll_rows(sides[7], 1))]
        + sides
        + [jnp.where(rows % 4 == 3, above, roll_rows(sides[0], -1))]
    )
    return centre, sides


def smooth(centre, sides):
    lanes = lax.broadcasted_iota(jnp.int32, TILE, 1)
    across = [c + 0.5 * (roll_rows(c, 4) + s) for c, s in zip(centre, sides)]
    out = []
    for v in range(SLICES):
        z = across[v + 1] + 0.5 * (across[v] + across[v + 2])
        up = jnp.where(lanes < 127, pltpu.roll(z, 127, 1), 0.0)
        down = jnp.where(lanes > 0, pltpu.roll(z, 1, 1), 0.0)
        out.append(z + 0.5 * (up + down))
    return out


def stencil(field, visc, weight):
    centre, sides = field
    visc_centre, visc_sides = visc
    flat = smooth(centre, sides)
    scaled = smooth(
        [a * b for a, b in zip(visc_centre, centre)], [a * b for a, b in zip(visc_sides, sides)]
    )
    return [
        (1.0 / 3.0) * (centre[v + 1] * weight[v] - visc_centre[v + 1] * flat[v] - scaled[v])
        for v in range(SLICES)
    ]


def stencil_weight(visc):
    flat = smooth(*visc)
    return [8.0 * visc[0][v + 1] + flat[v] for v in range(SLICES)]


def sym_inverse(d):
    a, b, c, e, f, g = d
    c00, c01, c02 = e * g - f * f, c * f - b * g, b * f - c * e
    r = 1.0 / (a * c00 + b * c01 + c * c02)
    return [r * q for q in (c00, c01, c02, a * g - c * c, b * c - a * f, a * e - b * b)]


def dot3(xs, ys):
    return xs[0] * ys[0] + xs[1] * ys[1] + xs[2] * ys[2]


def mat_vec(m, x):
    return [dot3(m[i], x) for i in range(3)]


def mat_mat(m, n):
    return [[dot3(m[i], [n[0][j], n[1][j], n[2][j]]) for j in range(3)] for i in range(3)]


def sym_product(m, n):
    return [dot3(m[i], [n[0][j], n[1][j], n[2][j]]) for i in range(3) for j in range(i, 3)]


def transposed(m):
    return [[m[j][i] for j in range(3)] for i in range(3)]


def full(d):
    return [[d[SYM[i][j]] for j in range(3)] for i in range(3)]


def eliminate(diag, to_prev, next_to):
    inv = full(sym_inverse(diag))
    pm = mat_mat(inv, to_prev)
    qm = mat_mat(inv, transposed(next_to))
    to_p = sym_product(transposed(to_prev), pm)
    return (inv, pm, qm), to_p, sym_product(next_to, qm), mat_mat(next_to, pm)


def push(done, source):
    inv, pm, qm = done
    return mat_vec(inv, source), mat_vec(transposed(pm), source), mat_vec(transposed(qm), source)


def back(done, y, x_prev, x_next):
    _, pm, qm = done
    return [y[i] + dot3(pm[i], x_prev) + dot3(qm[i], x_next) for i in range(3)]


def minus(a, b):
    return [x - y for x, y in zip(a, b)]


def plus(a, b):
    return [x + y for x, y in zip(a, b)]


def select(mask, a, b):
    return [jnp.where(mask, x, y) for x, y in zip(a, b)]


def keep(mask, a):
    return [jnp.where(mask, x, 0.0) for x in a]


def moved(a, shift):
    return [roll_rows(x, shift) for x in a]


def moved_mat(m, shift):
    return [moved(r, shift) for r in m]


def reduce_matrix(diag, link, pos):
    done4, to_p, to_n, passed = eliminate(diag, link, moved_mat(link, -1))
    base = keep(pos == 0, to_p)
    diag = minus(diag, plus(moved(to_n, 1), keep(pos == 1, moved(to_p, -1))))
    link = moved_mat(passed, 1)
    done5, to_p, to_n, passed = eliminate(diag, link, moved_mat(link, -2))
    base = plus(base, keep(pos == 0, moved(to_p, -1)))
    return done4, done5, base, minus(diag, moved(to_n, 2)), moved_mat(passed, 2)


def reduce_source(done4, done5, source, pos):
    y4, to_p, to_n = push(done4, source)
    base = keep(pos == 0, to_p)
    source = plus(source, plus(moved(to_n, 1), keep(pos == 1, moved(to_p, -1))))
    y5, to_p, to_n = push(done5, source)
    base = plus(base, keep(pos == 0, moved(to_p, -1)))
    return y4, y5, base, plus(source, moved(to_n, 2))


def expand_rows(done4, done5, y4, y5, x_base, x_last, pos):
    x_one = back(done5, y5, moved(x_base, 1), moved(x_last, -2))
    kept = select(pos == 1, x_one, x_last)
    x_even = back(done4, y4, select(pos == 0, x_base, moved(kept, 1)), moved(kept, -1))
    return select(pos % 2 == 0, x_even, kept)


ORDER = ((1, 0), (1, 2), (1, 4), (1, 6), (2, 1), (2, 5), (4, 3))


def solve_kernel(
    tiles, groups, vel_in, force_in, visc_in, fibre_in, mass_in,
    update, ends, visc_out, rx_left, rx_right,
    vel, force, visc, fibre, mass, tx_left, tx_right, tx_top, tx_bot,
    h_left, h_right, h_below, h_rest, matrix_own, matrix_all, source_own, source_all,
    ux_left, ux_right, load_sems, halo_send, halo_recv, mat_send, mat_recv, src_send, src_recv,
    upd_send, upd_recv,
):
    t, k = lax.axis_index("tile"), lax.axis_index("thick")
    loads = [
        pltpu.make_async_copy(src, dst, load_sems.at[i])
        for i, (src, dst) in enumerate(
            ((visc_in, visc), (fibre_in, fibre), (vel_in, vel), (mass_in, mass), (force_in, force))
        )
    ]
    for load in loads:
        load.start()
    has_left, has_right, has_down, has_up = t > 0, t < tiles - 1, k > 0, k < groups - 1
    left, right = jnp.maximum(t - 1, 0), jnp.minimum(t + 1, tiles - 1)
    down, up = jnp.maximum(k - 1, 0), jnp.minimum(k + 1, groups - 1)
    both = jnp.logical_and
    peers = [(t, lax.rem(k + d, groups)) for d in range(1, groups)]
    corner = tx_top.at[pl.ds(0, 1)]
    rest = [h_rest.at[pl.ds(i, 1)] for i in range(5)]
    plan = [
        ((t, up), has_up, has_down, tx_top, h_below),
        ((t, down), has_down, has_up, tx_bot, rest[0]),
        ((left, k), has_left, has_right, tx_left, h_right),
        ((right, k), has_right, has_left, tx_right, h_left),
        ((right, up), both(has_right, has_up), both(has_left, has_down), corner, rest[1]),
        ((left, up), both(has_left, has_up), both(has_right, has_down), corner, rest[2]),
        ((right, down), both(has_right, has_down), both(has_left, has_up), tx_bot, rest[3]),
        ((left, down), both(has_left, has_down), both(has_right, has_up), tx_bot, rest[4]),
    ]
    all_here = greet([(p[0], p[1]) for p in plan[2:]] + [(p, None) for p in peers])
    halo = [
        (there, comes, remote(src, dst, halo_send.at[i], halo_recv.at[i], target))
        for i, (target, there, comes, src, dst) in enumerate(plan)
    ]
    for load in loads[:3]:
        load.wait()
    visc_c = load_slices(visc)
    fib = [load_slices(fibre, (c,)) for c in range(3)]
    v_c = [load_slices(vel, (c,)) for c in range(3)]
    fields = v_c + [visc_c]
    tx_bot[0] = pack_rows([f[0] for f in fields], 0)
    tx_top[0] = pack_rows([f[7] for f in fields], 3)
    tx_top[1] = pack_rows([f[7] for f in fib], 3)
    pack_sides(tx_left, tx_right, fields)
    all_here()
    for there, _, copy in halo:
        when(there, copy.start)
    place = edges(tiles, groups)
    rows, low, side_ok, has_below, has_above = place
    pos = rows % 4
    inner = pos < 3
    loads[3].wait()
    loads[4].wait()
    mass_c = load_slices(mass)
    for _, comes, copy in halo[:2]:
        when(comes, copy.wait_recv)
    centre = (
        [below_slice(visc_c, h_below[0], 3, has_below, rows)]
        + visc_c
        + [above_slice(visc_c, h_rest[0], 3, has_above, rows)]
    )
    fib = [[below_slice(fib[c], h_below[1], c, has_below, rows)] + fib[c] for c in range(3)]
    face = []
    for v in range(SLICES + 1):
        mu = 0.5 * (centre[v] + centre[v + 1])
        f = [fib[c][v] for c in range(3)]
        g = [mu * q for q in f]
        face.append(
            [mu + g[0] * f[0], g[0] * f[1], g[0] * f[2], mu + g[1] * f[1], g[1] * f[2], mu + g[2] * f[2]]
        )
    diag, link = [], []
    for v in range(SLICES):
        d = plus(face[v], face[v + 1])
        m = mass_c[v] * centre[v + 1]
        for i in (0, 3, 5):
            d[i] = d[i] + m
        diag.append(d)
        link.append(full(face[v]))
    top_diag = diag[7]
    joined = jnp.logical_or(pos > 0, has_below)
    link[0] = [keep(joined, r) for r in link[0]]
    done = []
    low_d = None
    for step, e in ORDER:
        n, p = e + step, e - step
        solved, to_p, to_n, passed = eliminate(diag[e], link[e], link[n])
        done.append(solved)
        diag[n], link[n] = minus(diag[n], to_n), passed
        if p >= 0:
            diag[p] = minus(diag[p], to_p)
        else:
            low_d = to_p if low_d is None else plus(low_d, to_p)
    d7 = minus(diag[7], keep(inner, moved(low_d, -1)))
    done4, done5, base_d, last_d, last_l = reduce_matrix(d7, link[7], pos)
    out = moved(plus(base_d, low_d), 3) + last_d + [e for r in last_l for e in r]
    for i in range(6):
        matrix_own[i] = pack_rows(out[4 * i : 4 * i + 4], 3)
    mat_copies = [
        remote(matrix_own, matrix_all.at[k], mat_send.at[i], mat_recv.at[i], p)
        for i, p in enumerate(peers)
    ]
    for copy in mat_copies:
        copy.start()
    matrix_all[k] = matrix_own[...]

    for _, comes, copy in halo[2:]:
        when(comes, copy.wait_recv)
    around = (h_left, h_right, h_below, h_rest, place)
    visc_ext = extended(visc_c, 3, *around)
    weight = stencil_weight(visc_ext)
    source = [[] for _ in range(SLICES)]
    for c in range(3):
        image = stencil(extended(v_c[c], c, *around), visc_ext, weight)
        force_c = load_slices(force, (c,))
        for v in range(SLICES):
            source[v].append(force_c[v] - image[v])
    top_source = source[7]
    ys = []
    low_s = None
    for (step, e), solved in zip(ORDER, done):
        n, p = e + step, e - step
        y, to_p, to_n = push(solved, source[e])
        ys.append(y)
        source[n] = plus(source[n], to_n)
        if p >= 0:
            source[p] = plus(source[p], to_p)
        else:
            low_s = to_p if low_s is None else plus(low_s, to_p)
    s7 = plus(source[7], keep(inner, moved(low_s, -1)))
    y4, y5, base_s, last_s = reduce_source(done4, done5, s7, pos)
    out = moved(plus(base_s, low_s), 3) + last_s
    source_own[0] = pack_rows(out[:4], 3)
    source_own[1] = pack_rows(out[4:], 3)
    src_copies = [
        remote(source_own, source_all.at[k], src_send.at[i], src_recv.at[i], p)
        for i, p in enumerate(peers)
    ]
    for copy in src_copies:
        copy.start()
    source_all[k] = source_own[...]
    for i in range(SLICES + 2):
        visc_out[i] = visc_ext[0][i]
        visc_out[SLICES + 2 + i] = visc_ext[1][i]
    for v in range(SLICES):
        visc_out[2 * SLICES + 4 + v] = weight[v]

    def gathered(ref, lo, hi, h):
        values = []
        for f in range(lo, hi):
            value = None
            for s in range(4):
                part = roll_rows(ref[2 * s + h, f // 4], s - f % 4)
                value = part if value is None else jnp.where(pos == s, part, value)
            values.append(value)
        return values

    def link_of(h):
        e = gathered(matrix_all, 12, 21, h)
        return [e[0:3], e[3:6], e[6:9]]

    for copy in mat_copies:
        copy.wait_recv()
    d0 = minus(gathered(matrix_all, 6, 12, 0), gathered(matrix_all, 0, 6, 1))
    d1 = minus(
        gathered(matrix_all, 6, 12, 1), keep(inner, moved(gathered(matrix_all, 0, 6, 0), -1))
    )
    r_h, to_p, to_n, passed = eliminate(d0, link_of(0), link_of(1))
    d1 = minus(minus(d1, to_n), keep(inner, moved(to_p, -1)))
    r4, r5, _, end_d, _ = reduce_matrix(d1, passed, pos)
    end_inv = full(sym_inverse(end_d))
    face_inv = full(sym_inverse(face[8]))
    for copy in src_copies:
        copy.wait_recv()
    s0 = plus(gathered(source_all, 3, 6, 0), gathered(source_all, 0, 3, 1))
    s1 = plus(
        gathered(source_all, 3, 6, 1), keep(inner, moved(gathered(source_all, 0, 3, 0), -1))
    )
    z_h, to_p, to_n = push(r_h, s0)
    s1 = plus(plus(s1, to_n), keep(inner, moved(to_p, -1)))
    z4, z5, _, end_s = reduce_source(r4, r5, s1, pos)
    nothing = [jnp.zeros(TILE, jnp.float32)] * 3
    x1 = expand_rows(r4, r5, z4, z5, nothing, mat_vec(end_inv, end_s), pos)
    x0 = back(r_h, z_h, keep(pos > 0, moved(x1, 1)), x1)
    own, base = nothing, nothing
    for g in range(groups):
        x = (x0, x1)[g % 2]
        own = select(k == g, moved(x, 3 - g // 2), own)
        base = select(k == g + 1, moved(x, -(g // 2)), base)
    x = [None] * SLICES
    x[7] = expand_rows(done4, done5, y4, y5, base, own, pos)
    under = select(pos == 0, base, moved(x[7], 1))
    for (step, e), solved, y in reversed(list(zip(ORDER, done, ys))):
        x[e] = back(solved, y, under if e < step else x[e - step], x[e + step])
    rhs = minus(mat_vec(full(top_diag), x[7]), mat_vec(full(face[7]), x[6]))
    over = keep(has_above, mat_vec(face_inv, minus(rhs, top_source)))
    pack_sides(ux_left, ux_right, [[x[v][c] for v in range(SLICES)] for c in range(3)])
    packed_base, packed_over = pack_rows(base, 0), pack_rows(over, 3)
    ux_left[12] = jnp.where(low, packed_base, roll_rows(packed_over, 4))
    ux_right[12] = jnp.where(low, roll_rows(packed_base, 4), packed_over)
    last = [
        (has_left, has_right, remote(ux_left, rx_right, upd_send.at[0], upd_recv.at[0], (left, k))),
        (has_right, has_left, remote(ux_right, rx_left, upd_send.at[1], upd_recv.at[1], (right, k))),
    ]
    for there, _, copy in last:
        when(there, copy.start)
    for c in range(3):
        for v in range(SLICES):
            update[8 * c + v] = x[v][c]
        ends[c] = base[c]
        ends[3 + c] = over[c]
    for there, _, copy in halo:
        when(there, copy.wait_send)
    for copy in mat_copies + src_copies:
        copy.wait_send()
    for there, comes, copy in last:
        when(comes, copy.wait_recv)
        when(there, copy.wait_send)


def image_kernel(tiles, groups, solved, ends, visc, rx_left, rx_right, update, image):
    rows, low, side_ok, has_below, has_above = edges(tiles, groups)
    pos = rows % 4
    visc_ext = ([visc[i] for i in range(10)], [visc[10 + i] for i in range(10)])
    weight = [visc[20 + v] for v in range(SLICES)]
    for c in range(3):
        x = [solved[8 * c + v] for v in range(SLICES)]
        store_slices(update, (c,), x)
        sides = []
        for m in range(4):
            lt, rt = rx_left[4 * c + m], rx_right[4 * c + m]
            sides.append(jnp.where(side_ok, jnp.where(low, lt, roll_rows(rt, 4)), 0.0))
            sides.append(jnp.where(side_ok, jnp.where(low, roll_rows(lt, 4), rt), 0.0))
        lt, rt = rx_left[12], rx_right[12]
        under = jnp.where(low, roll_rows(lt, -c), roll_rows(rt, 4 - c))
        over = jnp.where(low, roll_rows(lt, -1 - c), roll_rows(rt, 3 - c))
        centre = (
            [jnp.where(pos == 0, ends[c], roll_rows(x[7], 1))]
            + x
            + [jnp.where(pos == 3, ends[3 + c], roll_rows(x[0], -1))]
        )
        sides = (
            [jnp.where(pos == 0, jnp.where(side_ok, under, 0.0), roll_rows(sides[7], 1))]
            + sides
            + [jnp.where(pos == 3, jnp.where(side_ok, over, 0.0), roll_rows(sides[0], -1))]
        )
        store_slices(image, (c,), stencil((centre, sides), visc_ext, weight))


def tiles_of(*lead):
    return jax.ShapeDtypeStruct(lead + TILE, jnp.float32)


def per_device(tiles, groups, velocity, forcing, viscosity, fibre, inertia):
    vel, force, fib = (a.reshape(3, 64, 128) for a in (velocity, forcing, fibre))
    visc, mass = viscosity.reshape(64, 128), inertia.reshape(64, 128)
    bind = functools.partial
    vmem = pl.BlockSpec(memory_space=pltpu.VMEM)
    hbm = pl.BlockSpec(memory_space=pltpu.HBM)
    block = jax.ShapeDtypeStruct((3, 64, 128), jnp.float32)

    def space(*shape):
        return pltpu.VMEM(shape, jnp.float32)

    def tiles_in(*lead):
        return space(*lead, *TILE)

    dma = pltpu.SemaphoreType.DMA
    parts = pl.pallas_call(
        bind(solve_kernel, tiles, groups),
        out_shape=[tiles_of(n) for n in (24, 6, 28, 13, 13)],
        in_specs=[hbm] * 5,
        out_specs=[vmem] * 5,
        scratch_shapes=[
            space(3, 64, 128), space(3, 64, 128), space(64, 128), space(3, 64, 128), space(64, 128),
            tiles_in(16), tiles_in(16), tiles_in(2), tiles_in(1),
            tiles_in(16), tiles_in(16), tiles_in(2), tiles_in(5),
            tiles_in(6), tiles_in(groups, 6), tiles_in(2), tiles_in(groups, 2),
            tiles_in(13), tiles_in(13),
            dma((5,)), dma((8,)), dma((8,)),
            dma((groups - 1,)), dma((groups - 1,)), dma((groups - 1,)), dma((groups - 1,)),
            dma((2,)), dma((2,)),
        ],
        compiler_params=pltpu.CompilerParams(
            collective_id=0, has_side_effects=True, vmem_limit_bytes=67_000_000
        ),
        name="solve",
    )(vel, force, visc, fib, mass)
    update, image = pl.pallas_call(
        bind(image_kernel, tiles, groups),
        out_shape=[block, block],
        in_specs=[vmem] * 5,
        out_specs=[vmem] * 2,
        compiler_params=pltpu.CompilerParams(vmem_limit_bytes=67_000_000),
        name="image",
    )(*parts)
    return update.reshape(velocity.shape), image.reshape(velocity.shape)


def solution(mesh):
    wide, flat = P(None, "thick", "tile", None), P("thick", "tile", None)
    return jax.shard_map(
        functools.partial(per_device, mesh.shape["tile"], mesh.shape["thick"]),
        mesh=mesh,
        in_specs=(wide, wide, flat, wide, flat),
        out_specs=(wide, wide),
        check_vma=False,
    )
```

```python
import functools

import jax
import jax.numpy as jnp
from jax import lax
from jax.experimental import pallas as pl
from jax.experimental.pallas import tpu as pltpu
from jax.sharding import PartitionSpec as P

MESH = pl.DeviceIdType.MESH
SLICES = 8
SYM = ((0, 1, 2), (1, 3, 4), (2, 4, 5))
TILE = (8, 128)


def roll_rows(values, shift):
    return values if shift % 8 == 0 else pltpu.roll(values, shift % 8, 0)


def row_ids():
    return lax.broadcasted_iota(jnp.int32, TILE, 0)


def load_slices(ref, lead=()):
    def one(v):
        halves = [ref[lead + (pl.ds(2 * v + x, 4, stride=16), slice(None))] for x in (0, 1)]
        return jnp.concatenate(halves, axis=0)

    return [one(v) for v in range(SLICES)]


def store_slices(ref, lead, slices):
    for v in range(SLICES):
        for x in (0, 1):
            ref[lead + (pl.ds(2 * v + x, 4, stride=16), slice(None))] = slices[v][4 * x : 4 * x + 4]


def pack_rows(fields, pos):
    rows = row_ids() % 4
    packed = roll_rows(fields[0], -pos)
    for j in range(1, len(fields)):
        packed = jnp.where(rows == j, roll_rows(fields[j], j - pos), packed)
    return packed


def pack_sides(left_ref, right_ref, fields):
    low = row_ids() < 4
    for j, slices in enumerate(fields):
        for m in range(4):
            first, second = slices[2 * m], slices[2 * m + 1]
            left_ref[4 * j + m] = jnp.where(low, first, roll_rows(second, 4))
            right_ref[4 * j + m] = jnp.where(low, roll_rows(first, 4), second)


def greet(targets):
    barrier = pltpu.get_barrier_semaphore()
    count = 0
    for target, there in targets:
        if there is None:
            pl.semaphore_signal(barrier, inc=1, device_id=target, device_id_type=MESH)
            count = count + 1
        else:

            @pl.when(there)
            def _():
                pl.semaphore_signal(barrier, inc=1, device_id=target, device_id_type=MESH)

            count = count + there.astype(jnp.int32)
    return lambda: pl.semaphore_wait(barrier, count)


def remote(src, dst, send_sem, recv_sem, target):
    return pltpu.make_async_remote_copy(
        src_ref=src, dst_ref=dst, send_sem=send_sem, recv_sem=recv_sem,
        device_id=target, device_id_type=MESH,
    )


def when(there, action):
    pl.when(there)(lambda: action())


def edges(tiles, groups):
    t, k = lax.axis_index("tile"), lax.axis_index("thick")
    rows = row_ids()
    low = rows < 4
    side_ok = jnp.logical_or(
        jnp.logical_and(low, t > 0), jnp.logical_and(jnp.logical_not(low), t < tiles - 1)
    )
    return rows, low, side_ok, k > 0, k < groups - 1


def below_slice(slices, packed, j, has_below, rows):
    inside = roll_rows(slices[7], 1)
    return jnp.where(rows % 4 == 0, jnp.where(has_below, roll_rows(packed, -j), 0.0), inside)


def above_slice(slices, packed, j, has_above, rows):
    inside = roll_rows(slices[0], -1)
    return jnp.where(rows % 4 == 3, jnp.where(has_above, roll_rows(packed, 3 - j), 0.0), inside)


def extended(slices, j, rx_left, rx_right, rx_below, rx_rest, place):
    rows, low, side_ok, has_below, has_above = place
    sides = []
    for m in range(4):
        left, right = rx_left[4 * j + m], rx_right[4 * j + m]
        sides.append(jnp.where(side_ok, jnp.where(low, left, roll_rows(right, 4)), 0.0))
        sides.append(jnp.where(side_ok, jnp.where(low, roll_rows(left, 4), right), 0.0))
    centre = (
        [below_slice(slices, rx_below[0], j, has_below, rows)]
        + slices
        + [above_slice(slices, rx_rest[0], j, has_above, rows)]
    )
    below = roll_rows(jnp.where(low, rx_rest[2], rx_rest[1]), 4 - j)
    above = roll_rows(jnp.where(low, rx_rest[4], rx_rest[3]), 7 - j)
    below = jnp.where(jnp.logical_and(side_ok, has_below), below, 0.0)
    above = jnp.where(jnp.logical_and(side_ok, has_above), above, 0.0)
    sides = (
        [jnp.where(rows % 4 == 0, below, roll_rows(sides[7], 1))]
        + sides
        + [jnp.where(rows % 4 == 3, above, roll_rows(sides[0], -1))]
    )
    return centre, sides


def smooth(centre, sides):
    lanes = lax.broadcasted_iota(jnp.int32, TILE, 1)
    across = [c + 0.5 * (roll_rows(c, 4) + s) for c, s in zip(centre, sides)]
    out = []
    for v in range(SLICES):
        z = across[v + 1] + 0.5 * (across[v] + across[v + 2])
        up = jnp.where(lanes < 127, pltpu.roll(z, 127, 1), 0.0)
        down = jnp.where(lanes > 0, pltpu.roll(z, 1, 1), 0.0)
        out.append(z + 0.5 * (up + down))
    return out


def stencil(field, visc, weight):
    centre, sides = field
    visc_centre, visc_sides = visc
    flat = smooth(centre, sides)
    scaled = smooth(
        [a * b for a, b in zip(visc_centre, centre)], [a * b for a, b in zip(visc_sides, sides)]
    )
    return [
        (1.0 / 3.0) * (centre[v + 1] * weight[v] - visc_centre[v + 1] * flat[v] - scaled[v])
        for v in range(SLICES)
    ]


def stencil_weight(visc):
    flat = smooth(*visc)
    return [8.0 * visc[0][v + 1] + flat[v] for v in range(SLICES)]


def sym_inverse(d):
    a, b, c, e, f, g = d
    c00, c01, c02 = e * g - f * f, c * f - b * g, b * f - c * e
    r = 1.0 / (a * c00 + b * c01 + c * c02)
    return [r * q for q in (c00, c01, c02, a * g - c * c, b * c - a * f, a * e - b * b)]


def dot3(xs, ys):
    return xs[0] * ys[0] + xs[1] * ys[1] + xs[2] * ys[2]


def mat_vec(m, x):
    return [dot3(m[i], x) for i in range(3)]


def mat_mat(m, n):
    return [[dot3(m[i], [n[0][j], n[1][j], n[2][j]]) for j in range(3)] for i in range(3)]


def sym_product(m, n):
    return [dot3(m[i], [n[0][j], n[1][j], n[2][j]]) for i in range(3) for j in range(i, 3)]


def transposed(m):
    return [[m[j][i] for j in range(3)] for i in range(3)]


def full(d):
    return [[d[SYM[i][j]] for j in range(3)] for i in range(3)]


def eliminate(diag, to_prev, next_to):
    inv = full(sym_inverse(diag))
    pm = mat_mat(inv, to_prev)
    qm = mat_mat(inv, transposed(next_to))
    to_p = sym_product(transposed(to_prev), pm)
    return (inv, pm, qm), to_p, sym_product(next_to, qm), mat_mat(next_to, pm)


def push(done, source):
    inv, pm, qm = done
    return mat_vec(inv, source), mat_vec(transposed(pm), source), mat_vec(transposed(qm), source)


def back(done, y, x_prev, x_next):
    _, pm, qm = done
    return [y[i] + dot3(pm[i], x_prev) + dot3(qm[i], x_next) for i in range(3)]


def minus(a, b):
    return [x - y for x, y in zip(a, b)]


def plus(a, b):
    return [x + y for x, y in zip(a, b)]


def select(mask, a, b):
    return [jnp.where(mask, x, y) for x, y in zip(a, b)]


def keep(mask, a):
    return [jnp.where(mask, x, 0.0) for x in a]


def moved(a, shift):
    return [roll_rows(x, shift) for x in a]


def moved_mat(m, shift):
    return [moved(r, shift) for r in m]


def reduce_matrix(diag, link, pos):
    done4, to_p, to_n, passed = eliminate(diag, link, moved_mat(link, -1))
    base = keep(pos == 0, to_p)
    diag = minus(diag, plus(moved(to_n, 1), keep(pos == 1, moved(to_p, -1))))
    link = moved_mat(passed, 1)
    done5, to_p, to_n, passed = eliminate(diag, link, moved_mat(link, -2))
    base = plus(base, keep(pos == 0, moved(to_p, -1)))
    return done4, done5, base, minus(diag, moved(to_n, 2)), moved_mat(passed, 2)


def reduce_source(done4, done5, source, pos):
    y4, to_p, to_n = push(done4, source)
    base = keep(pos == 0, to_p)
    source = plus(source, plus(moved(to_n, 1), keep(pos == 1, moved(to_p, -1))))
    y5, to_p, to_n = push(done5, source)
    base = plus(base, keep(pos == 0, moved(to_p, -1)))
    return y4, y5, base, plus(source, moved(to_n, 2))


def expand_rows(done4, done5, y4, y5, x_base, x_last, pos):
    x_one = back(done5, y5, moved(x_base, 1), moved(x_last, -2))
    kept = select(pos == 1, x_one, x_last)
    x_even = back(done4, y4, select(pos == 0, x_base, moved(kept, 1)), moved(kept, -1))
    return select(pos % 2 == 0, x_even, kept)


ORDER = ((1, 0), (1, 2), (1, 4), (1, 6), (2, 1), (2, 5), (4, 3))


def solve_kernel(
    tiles, groups, vel_in, force_in, visc_in, fibre_in, mass_in,
    update, ends, visc_out, rx_left, rx_right,
    vel, force, visc, fibre, mass, tx_left, tx_right, tx_top, tx_bot,
    h_left, h_right, h_below, h_rest, matrix_own, matrix_all, source_own, source_all,
    ux_left, ux_right, load_sems, halo_send, halo_recv, mat_send, mat_recv, src_send, src_recv,
    upd_send, upd_recv, relay_send, relay_recv,
):
    t, k = lax.axis_index("tile"), lax.axis_index("thick")
    loads = [
        pltpu.make_async_copy(src, dst, load_sems.at[i])
        for i, (src, dst) in enumerate(
            ((visc_in, visc), (fibre_in, fibre), (vel_in, vel), (mass_in, mass), (force_in, force))
        )
    ]
    for load in loads:
        load.start()
    has_left, has_right, has_down, has_up = t > 0, t < tiles - 1, k > 0, k < groups - 1
    left, right = jnp.maximum(t - 1, 0), jnp.minimum(t + 1, tiles - 1)
    down, up = jnp.maximum(k - 1, 0), jnp.minimum(k + 1, groups - 1)
    both = jnp.logical_and
    half = groups // 2
    ring = [d for j in range(half, 0, -1) for d in sorted({j, groups - j})]
    peers = [(t, lax.rem(k + d, groups)) for d in ring]
    above, below = (t, lax.rem(k + 1, groups)), (t, lax.rem(k + groups - 1, groups))
    corner = tx_top.at[pl.ds(0, 1)]
    rest = [h_rest.at[pl.ds(i, 1)] for i in range(5)]
    plan = [
        ((t, up), has_up, has_down, tx_top, h_below),
        ((t, down), has_down, has_up, tx_bot, rest[0]),
        ((left, k), has_left, has_right, tx_left, h_right),
        ((right, k), has_right, has_left, tx_right, h_left),
        ((right, up), both(has_right, has_up), both(has_left, has_down), corner, rest[1]),
        ((left, up), both(has_left, has_up), both(has_right, has_down), corner, rest[2]),
        ((right, down), both(has_right, has_down), both(has_left, has_up), tx_bot, rest[3]),
        ((left, down), both(has_left, has_down), both(has_right, has_up), tx_bot, rest[4]),
    ]
    all_here = greet([(p[0], p[1]) for p in plan[2:]] + [(p, None) for p in peers])
    halo = [
        (there, comes, remote(src, dst, halo_send.at[i], halo_recv.at[i], target))
        for i, (target, there, comes, src, dst) in enumerate(plan)
    ]
    for load in loads[:3]:
        load.wait()
    visc_c = load_slices(visc)
    fib = [load_slices(fibre, (c,)) for c in range(3)]
    v_c = [load_slices(vel, (c,)) for c in range(3)]
    fields = v_c + [visc_c]
    tx_bot[0] = pack_rows([f[0] for f in fields], 0)
    tx_top[0] = pack_rows([f[7] for f in fields], 3)
    tx_top[1] = pack_rows([f[7] for f in fib], 3)
    pack_sides(tx_left, tx_right, fields)
    all_here()
    for there, _, copy in halo:
        when(there, copy.start)
    place = edges(tiles, groups)
    rows, low, side_ok, has_below, has_above = place
    pos = rows % 4
    inner = pos < 3
    loads[3].wait()
    loads[4].wait()
    mass_c = load_slices(mass)
    for _, comes, copy in halo[:2]:
        when(comes, copy.wait_recv)
    centre = (
        [below_slice(visc_c, h_below[0], 3, has_below, rows)]
        + visc_c
        + [above_slice(visc_c, h_rest[0], 3, has_above, rows)]
    )
    fib = [[below_slice(fib[c], h_below[1], c, has_below, rows)] + fib[c] for c in range(3)]
    face = []
    for v in range(SLICES + 1):
        mu = 0.5 * (centre[v] + centre[v + 1])
        f = [fib[c][v] for c in range(3)]
        g = [mu * q for q in f]
        face.append(
            [mu + g[0] * f[0], g[0] * f[1], g[0] * f[2], mu + g[1] * f[1], g[1] * f[2], mu + g[2] * f[2]]
        )
    diag, link = [], []
    for v in range(SLICES):
        d = plus(face[v], face[v + 1])
        m = mass_c[v] * centre[v + 1]
        for i in (0, 3, 5):
            d[i] = d[i] + m
        diag.append(d)
        link.append(full(face[v]))
    top_diag = diag[7]
    joined = jnp.logical_or(pos > 0, has_below)
    link[0] = [keep(joined, r) for r in link[0]]
    done = []
    low_d = None
    for step, e in ORDER:
        n, p = e + step, e - step
        solved, to_p, to_n, passed = eliminate(diag[e], link[e], link[n])
        done.append(solved)
        diag[n], link[n] = minus(diag[n], to_n), passed
        if p >= 0:
            diag[p] = minus(diag[p], to_p)
        else:
            low_d = to_p if low_d is None else plus(low_d, to_p)
    d7 = minus(diag[7], keep(inner, moved(low_d, -1)))
    done4, done5, base_d, last_d, last_l = reduce_matrix(d7, link[7], pos)
    out = moved(plus(base_d, low_d), 3) + last_d + [e for r in last_l for e in r]
    for i in range(6):
        matrix_own[i] = pack_rows(out[4 * i : 4 * i + 4], 3)
    mat_copies = [
        remote(matrix_own, matrix_all.at[k], mat_send.at[i], mat_recv.at[i], p)
        for i, p in enumerate(peers[1:])
    ]
    passed_up = matrix_all.at[lax.rem(k + groups - half + 1, groups), pl.ds(0, 3)]
    passed_down = matrix_all.at[lax.rem(k + half - 1, groups), pl.ds(3, 3)]
    relays = [
        remote(passed_up, passed_up, relay_send.at[0], relay_recv.at[0], above),
        remote(passed_down, passed_down, relay_send.at[1], relay_recv.at[1], below),
    ]
    for copy in mat_copies:
        copy.start()
    matrix_all[k] = matrix_own[...]

    for _, comes, copy in halo[2:]:
        when(comes, copy.wait_recv)
    around = (h_left, h_right, h_below, h_rest, place)
    visc_ext = extended(visc_c, 3, *around)
    weight = stencil_weight(visc_ext)
    source = [[] for _ in range(SLICES)]
    for c in range(3):
        image = stencil(extended(v_c[c], c, *around), visc_ext, weight)
        force_c = load_slices(force, (c,))
        for v in range(SLICES):
            source[v].append(force_c[v] - image[v])
    top_source = source[7]
    ys = []
    low_s = None
    for (step, e), solved in zip(ORDER, done):
        n, p = e + step, e - step
        y, to_p, to_n = push(solved, source[e])
        ys.append(y)
        source[n] = plus(source[n], to_n)
        if p >= 0:
            source[p] = plus(source[p], to_p)
        else:
            low_s = to_p if low_s is None else plus(low_s, to_p)
    s7 = plus(source[7], keep(inner, moved(low_s, -1)))
    y4, y5, base_s, last_s = reduce_source(done4, done5, s7, pos)
    out = moved(plus(base_s, low_s), 3) + last_s
    source_own[0] = pack_rows(out[:4], 3)
    source_own[1] = pack_rows(out[4:], 3)
    src_copies = [
        remote(source_own, source_all.at[k], src_send.at[i], src_recv.at[i], p)
        for i, p in enumerate(peers)
    ]
    for copy in src_copies:
        copy.start()
    source_all[k] = source_own[...]
    for i in range(SLICES + 2):
        visc_out[i] = visc_ext[0][i]
        visc_out[SLICES + 2 + i] = visc_ext[1][i]
    for v in range(SLICES):
        visc_out[2 * SLICES + 4 + v] = weight[v]

    for copy, relay in zip(mat_copies[:2], relays):
        copy.wait_recv()
        relay.start()

    def gathered(ref, lo, hi, h):
        values = []
        for f in range(lo, hi):
            value = None
            for s in range(4):
                part = roll_rows(ref[2 * s + h, f // 4], s - f % 4)
                value = part if value is None else jnp.where(pos == s, part, value)
            values.append(value)
        return values

    def link_of(h):
        e = gathered(matrix_all, 12, 21, h)
        return [e[0:3], e[3:6], e[6:9]]

    for copy in mat_copies[2:] + relays:
        copy.wait_recv()
    d0 = minus(gathered(matrix_all, 6, 12, 0), gathered(matrix_all, 0, 6, 1))
    d1 = minus(
        gathered(matrix_all, 6, 12, 1), keep(inner, moved(gathered(matrix_all, 0, 6, 0), -1))
    )
    r_h, to_p, to_n, passed = eliminate(d0, link_of(0), link_of(1))
    d1 = minus(minus(d1, to_n), keep(inner, moved(to_p, -1)))
    r4, r5, _, end_d, _ = reduce_matrix(d1, passed, pos)
    end_inv = full(sym_inverse(end_d))
    face_inv = full(sym_inverse(face[8]))
    for copy in src_copies:
        copy.wait_recv()
    s0 = plus(gathered(source_all, 3, 6, 0), gathered(source_all, 0, 3, 1))
    s1 = plus(
        gathered(source_all, 3, 6, 1), keep(inner, moved(gathered(source_all, 0, 3, 0), -1))
    )
    z_h, to_p, to_n = push(r_h, s0)
    s1 = plus(plus(s1, to_n), keep(inner, moved(to_p, -1)))
    z4, z5, _, end_s = reduce_source(r4, r5, s1, pos)
    nothing = [jnp.zeros(TILE, jnp.float32)] * 3
    x1 = expand_rows(r4, r5, z4, z5, nothing, mat_vec(end_inv, end_s), pos)
    x0 = back(r_h, z_h, keep(pos > 0, moved(x1, 1)), x1)
    own, base = nothing, nothing
    for g in range(groups):
        x = (x0, x1)[g % 2]
        own = select(k == g, moved(x, 3 - g // 2), own)
        base = select(k == g + 1, moved(x, -(g // 2)), base)
    x = [None] * SLICES
    x[7] = expand_rows(done4, done5, y4, y5, base, own, pos)
    under = select(pos == 0, base, moved(x[7], 1))
    for (step, e), solved, y in reversed(list(zip(ORDER, done, ys))):
        x[e] = back(solved, y, under if e < step else x[e - step], x[e + step])
    rhs = minus(mat_vec(full(top_diag), x[7]), mat_vec(full(face[7]), x[6]))
    over = keep(has_above, mat_vec(face_inv, minus(rhs, top_source)))
    pack_sides(ux_left, ux_right, [[x[v][c] for v in range(SLICES)] for c in range(3)])
    packed_base, packed_over = pack_rows(base, 0), pack_rows(over, 3)
    ux_left[12] = jnp.where(low, packed_base, roll_rows(packed_over, 4))
    ux_right[12] = jnp.where(low, roll_rows(packed_base, 4), packed_over)
    last = [
        (has_left, has_right, remote(ux_left, rx_right, upd_send.at[0], upd_recv.at[0], (left, k))),
        (has_right, has_left, remote(ux_right, rx_left, upd_send.at[1], upd_recv.at[1], (right, k))),
    ]
    for there, _, copy in last:
        when(there, copy.start)
    for c in range(3):
        for v in range(SLICES):
            update[8 * c + v] = x[v][c]
        ends[c] = base[c]
        ends[3 + c] = over[c]
    for there, _, copy in halo:
        when(there, copy.wait_send)
    for copy in mat_copies + relays + src_copies:
        copy.wait_send()
    for there, comes, copy in last:
        when(comes, copy.wait_recv)
        when(there, copy.wait_send)


def image_kernel(tiles, groups, solved, ends, visc, rx_left, rx_right, update, image):
    rows, low, side_ok, has_below, has_above = edges(tiles, groups)
    pos = rows % 4
    visc_ext = ([visc[i] for i in range(10)], [visc[10 + i] for i in range(10)])
    weight = [visc[20 + v] for v in range(SLICES)]
    for c in range(3):
        x = [solved[8 * c + v] for v in range(SLICES)]
        store_slices(update, (c,), x)
        sides = []
        for m in range(4):
            lt, rt = rx_left[4 * c + m], rx_right[4 * c + m]
            sides.append(jnp.where(side_ok, jnp.where(low, lt, roll_rows(rt, 4)), 0.0))
            sides.append(jnp.where(side_ok, jnp.where(low, roll_rows(lt, 4), rt), 0.0))
        lt, rt = rx_left[12], rx_right[12]
        under = jnp.where(low, roll_rows(lt, -c), roll_rows(rt, 4 - c))
        over = jnp.where(low, roll_rows(lt, -1 - c), roll_rows(rt, 3 - c))
        centre = (
            [jnp.where(pos == 0, ends[c], roll_rows(x[7], 1))]
            + x
            + [jnp.where(pos == 3, ends[3 + c], roll_rows(x[0], -1))]
        )
        sides = (
            [jnp.where(pos == 0, jnp.where(side_ok, under, 0.0), roll_rows(sides[7], 1))]
            + sides
            + [jnp.where(pos == 3, jnp.where(side_ok, over, 0.0), roll_rows(sides[0], -1))]
        )
        store_slices(image, (c,), stencil((centre, sides), visc_ext, weight))


def tiles_of(*lead):
    return jax.ShapeDtypeStruct(lead + TILE, jnp.float32)


def per_device(tiles, groups, velocity, forcing, viscosity, fibre, inertia):
    vel, force, fib = (a.reshape(3, 64, 128) for a in (velocity, forcing, fibre))
    visc, mass = viscosity.reshape(64, 128), inertia.reshape(64, 128)
    bind = functools.partial
    vmem = pl.BlockSpec(memory_space=pltpu.VMEM)
    hbm = pl.BlockSpec(memory_space=pltpu.HBM)
    block = jax.ShapeDtypeStruct((3, 64, 128), jnp.float32)

    def space(*shape):
        return pltpu.VMEM(shape, jnp.float32)

    def tiles_in(*lead):
        return space(*lead, *TILE)

    dma = pltpu.SemaphoreType.DMA
    parts = pl.pallas_call(
        bind(solve_kernel, tiles, groups),
        out_shape=[tiles_of(n) for n in (24, 6, 28, 13, 13)],
        in_specs=[hbm] * 5,
        out_specs=[vmem] * 5,
        scratch_shapes=[
            space(3, 64, 128), space(3, 64, 128), space(64, 128), space(3, 64, 128), space(64, 128),
            tiles_in(16), tiles_in(16), tiles_in(2), tiles_in(1),
            tiles_in(16), tiles_in(16), tiles_in(2), tiles_in(5),
            tiles_in(6), tiles_in(groups, 6), tiles_in(2), tiles_in(groups, 2),
            tiles_in(13), tiles_in(13),
            dma((5,)), dma((8,)), dma((8,)),
            dma((groups - 2,)), dma((groups - 2,)), dma((groups - 1,)), dma((groups - 1,)),
            dma((2,)), dma((2,)), dma((2,)), dma((2,)),
        ],
        compiler_params=pltpu.CompilerParams(
            collective_id=0, has_side_effects=True, vmem_limit_bytes=67_000_000
        ),
        name="solve",
    )(vel, force, visc, fib, mass)
    update, image = pl.pallas_call(
        bind(image_kernel, tiles, groups),
        out_shape=[block, block],
        in_specs=[vmem] * 5,
        out_specs=[vmem] * 2,
        compiler_params=pltpu.CompilerParams(vmem_limit_bytes=67_000_000),
        name="image",
    )(*parts)
    return update.reshape(velocity.shape), image.reshape(velocity.shape)


def solution(mesh):
    wide, flat = P(None, "thick", "tile", None), P("thick", "tile", None)
    return jax.shard_map(
        functools.partial(per_device, mesh.shape["tile"], mesh.shape["thick"]),
        mesh=mesh,
        in_specs=(wide, wide, flat, wide, flat),
        out_specs=(wide, wide),
        check_vma=False,
    )
```

```python
import functools

import jax
import jax.numpy as jnp
from jax import lax
from jax.experimental import pallas as pl
from jax.experimental.pallas import tpu as pltpu
from jax.sharding import PartitionSpec as P

MESH = pl.DeviceIdType.MESH
SLICES = 8
SYM = ((0, 1, 2), (1, 3, 4), (2, 4, 5))
TILE = (8, 128)


def roll_rows(values, shift):
    return values if shift % 8 == 0 else pltpu.roll(values, shift % 8, 0)


def row_ids():
    return lax.broadcasted_iota(jnp.int32, TILE, 0)


def load_slices(ref, lead=()):
    def one(v):
        halves = [ref[lead + (pl.ds(2 * v + x, 4, stride=16), slice(None))] for x in (0, 1)]
        return jnp.concatenate(halves, axis=0)

    return [one(v) for v in range(SLICES)]


def store_slices(ref, lead, slices):
    for v in range(SLICES):
        for x in (0, 1):
            ref[lead + (pl.ds(2 * v + x, 4, stride=16), slice(None))] = slices[v][4 * x : 4 * x + 4]


def pack_rows(fields, pos):
    rows = row_ids() % 4
    packed = roll_rows(fields[0], -pos)
    for j in range(1, len(fields)):
        packed = jnp.where(rows == j, roll_rows(fields[j], j - pos), packed)
    return packed


def pack_sides(left_ref, right_ref, fields):
    low = row_ids() < 4
    for j, slices in enumerate(fields):
        for m in range(4):
            first, second = slices[2 * m], slices[2 * m + 1]
            left_ref[4 * j + m] = jnp.where(low, first, roll_rows(second, 4))
            right_ref[4 * j + m] = jnp.where(low, roll_rows(first, 4), second)


def greet(targets):
    barrier = pltpu.get_barrier_semaphore()
    count = 0
    for target, there in targets:
        if there is None:
            pl.semaphore_signal(barrier, inc=1, device_id=target, device_id_type=MESH)
            count = count + 1
        else:

            @pl.when(there)
            def _():
                pl.semaphore_signal(barrier, inc=1, device_id=target, device_id_type=MESH)

            count = count + there.astype(jnp.int32)
    return lambda: pl.semaphore_wait(barrier, count)


def remote(src, dst, send_sem, recv_sem, target):
    return pltpu.make_async_remote_copy(
        src_ref=src, dst_ref=dst, send_sem=send_sem, recv_sem=recv_sem,
        device_id=target, device_id_type=MESH,
    )


def when(there, action):
    pl.when(there)(lambda: action())


def edges(tiles, groups):
    t, k = lax.axis_index("tile"), lax.axis_index("thick")
    rows = row_ids()
    low = rows < 4
    side_ok = jnp.logical_or(
        jnp.logical_and(low, t > 0), jnp.logical_and(jnp.logical_not(low), t < tiles - 1)
    )
    return rows, low, side_ok, k > 0, k < groups - 1


def below_slice(slices, packed, j, has_below, rows):
    inside = roll_rows(slices[7], 1)
    return jnp.where(rows % 4 == 0, jnp.where(has_below, roll_rows(packed, -j), 0.0), inside)


def above_slice(slices, packed, j, has_above, rows):
    inside = roll_rows(slices[0], -1)
    return jnp.where(rows % 4 == 3, jnp.where(has_above, roll_rows(packed, 3 - j), 0.0), inside)


def extended(slices, j, rx_left, rx_right, rx_below, rx_rest, place):
    rows, low, side_ok, has_below, has_above = place
    sides = []
    for m in range(4):
        left, right = rx_left[4 * j + m], rx_right[4 * j + m]
        sides.append(jnp.where(side_ok, jnp.where(low, left, roll_rows(right, 4)), 0.0))
        sides.append(jnp.where(side_ok, jnp.where(low, roll_rows(left, 4), right), 0.0))
    centre = (
        [below_slice(slices, rx_below[0], j, has_below, rows)]
        + slices
        + [above_slice(slices, rx_rest[0], j, has_above, rows)]
    )
    below = roll_rows(jnp.where(low, rx_rest[2], rx_rest[1]), 4 - j)
    above = roll_rows(jnp.where(low, rx_rest[4], rx_rest[3]), 7 - j)
    below = jnp.where(jnp.logical_and(side_ok, has_below), below, 0.0)
    above = jnp.where(jnp.logical_and(side_ok, has_above), above, 0.0)
    sides = (
        [jnp.where(rows % 4 == 0, below, roll_rows(sides[7], 1))]
        + sides
        + [jnp.where(rows % 4 == 3, above, roll_rows(sides[0], -1))]
    )
    return centre, sides


def smooth(centre, sides):
    lanes = lax.broadcasted_iota(jnp.int32, TILE, 1)
    across = [c + 0.5 * (roll_rows(c, 4) + s) for c, s in zip(centre, sides)]
    out = []
    for v in range(SLICES):
        z = across[v + 1] + 0.5 * (across[v] + across[v + 2])
        up = jnp.where(lanes < 127, pltpu.roll(z, 127, 1), 0.0)
        down = jnp.where(lanes > 0, pltpu.roll(z, 1, 1), 0.0)
        out.append(z + 0.5 * (up + down))
    return out


def stencil(field, visc, weight):
    centre, sides = field
    visc_centre, visc_sides = visc
    flat = smooth(centre, sides)
    scaled = smooth(
        [a * b for a, b in zip(visc_centre, centre)], [a * b for a, b in zip(visc_sides, sides)]
    )
    return [
        (1.0 / 3.0) * (centre[v + 1] * weight[v] - visc_centre[v + 1] * flat[v] - scaled[v])
        for v in range(SLICES)
    ]


def stencil_weight(visc):
    flat = smooth(*visc)
    return [8.0 * visc[0][v + 1] + flat[v] for v in range(SLICES)]


def sym_inverse(d):
    a, b, c, e, f, g = d
    c00, c01, c02 = e * g - f * f, c * f - b * g, b * f - c * e
    r = 1.0 / (a * c00 + b * c01 + c * c02)
    return [r * q for q in (c00, c01, c02, a * g - c * c, b * c - a * f, a * e - b * b)]


def dot3(xs, ys):
    return xs[0] * ys[0] + xs[1] * ys[1] + xs[2] * ys[2]


def mat_vec(m, x):
    return [dot3(m[i], x) for i in range(3)]


def mat_mat(m, n):
    return [[dot3(m[i], [n[0][j], n[1][j], n[2][j]]) for j in range(3)] for i in range(3)]


def sym_product(m, n):
    return [dot3(m[i], [n[0][j], n[1][j], n[2][j]]) for i in range(3) for j in range(i, 3)]


def transposed(m):
    return [[m[j][i] for j in range(3)] for i in range(3)]


def full(d):
    return [[d[SYM[i][j]] for j in range(3)] for i in range(3)]


def eliminate(diag, to_prev, next_to):
    inv = full(sym_inverse(diag))
    pm = mat_mat(inv, to_prev)
    qm = mat_mat(inv, transposed(next_to))
    to_p = sym_product(transposed(to_prev), pm)
    return (inv, pm, qm), to_p, sym_product(next_to, qm), mat_mat(next_to, pm)


def push(done, source):
    inv, pm, qm = done
    return mat_vec(inv, source), mat_vec(transposed(pm), source), mat_vec(transposed(qm), source)


def back(done, y, x_prev, x_next):
    _, pm, qm = done
    return [y[i] + dot3(pm[i], x_prev) + dot3(qm[i], x_next) for i in range(3)]


def minus(a, b):
    return [x - y for x, y in zip(a, b)]


def plus(a, b):
    return [x + y for x, y in zip(a, b)]


def select(mask, a, b):
    return [jnp.where(mask, x, y) for x, y in zip(a, b)]


def keep(mask, a):
    return [jnp.where(mask, x, 0.0) for x in a]


def moved(a, shift):
    return [roll_rows(x, shift) for x in a]


def moved_mat(m, shift):
    return [moved(r, shift) for r in m]


def reduce_matrix(diag, link, pos):
    done4, to_p, to_n, passed = eliminate(diag, link, moved_mat(link, -1))
    base = keep(pos == 0, to_p)
    diag = minus(diag, plus(moved(to_n, 1), keep(pos == 1, moved(to_p, -1))))
    link = moved_mat(passed, 1)
    done5, to_p, to_n, passed = eliminate(diag, link, moved_mat(link, -2))
    base = plus(base, keep(pos == 0, moved(to_p, -1)))
    return done4, done5, base, minus(diag, moved(to_n, 2)), moved_mat(passed, 2)


def reduce_source(done4, done5, source, pos):
    y4, to_p, to_n = push(done4, source)
    base = keep(pos == 0, to_p)
    source = plus(source, plus(moved(to_n, 1), keep(pos == 1, moved(to_p, -1))))
    y5, to_p, to_n = push(done5, source)
    base = plus(base, keep(pos == 0, moved(to_p, -1)))
    return y4, y5, base, plus(source, moved(to_n, 2))


def expand_rows(done4, done5, y4, y5, x_base, x_last, pos):
    x_one = back(done5, y5, moved(x_base, 1), moved(x_last, -2))
    kept = select(pos == 1, x_one, x_last)
    x_even = back(done4, y4, select(pos == 0, x_base, moved(kept, 1)), moved(kept, -1))
    return select(pos % 2 == 0, x_even, kept)


ORDER = ((1, 0), (1, 2), (1, 4), (1, 6), (2, 1), (2, 5), (4, 3))


def solve_kernel(
    tiles, groups, vel_in, force_in, visc_in, fibre_in, mass_in,
    update, ends, visc_out, rx_left, rx_right,
    vel, force, visc, fibre, mass, tx_left, tx_right, tx_top, tx_bot,
    h_left, h_right, h_below, h_rest, matrix_own, matrix_all, source_own, source_all,
    ux_left, ux_right, load_sems, halo_send, halo_recv, mat_send, mat_recv, src_send, src_recv,
    upd_send, upd_recv, relay_send, relay_recv, reach_sems,
):
    t, k = lax.axis_index("tile"), lax.axis_index("thick")
    loads = [
        pltpu.make_async_copy(src, dst, load_sems.at[i])
        for i, (src, dst) in enumerate(
            ((visc_in, visc), (fibre_in, fibre), (vel_in, vel), (mass_in, mass), (force_in, force))
        )
    ]
    for load in loads:
        load.start()
    has_left, has_right, has_down, has_up = t > 0, t < tiles - 1, k > 0, k < groups - 1
    left, right = jnp.maximum(t - 1, 0), jnp.minimum(t + 1, tiles - 1)
    down, up = jnp.maximum(k - 1, 0), jnp.minimum(k + 1, groups - 1)
    both = jnp.logical_and
    half = groups // 2
    ring = [d for j in range(half, 0, -1) for d in sorted({j, groups - j})]
    peers = [(t, lax.rem(k + d, groups)) for d in ring]
    above, below = (t, lax.rem(k + 1, groups)), (t, lax.rem(k + groups - 1, groups))
    corner = tx_top.at[pl.ds(0, 1)]
    rest = [h_rest.at[pl.ds(i, 1)] for i in range(5)]
    plan = [
        ((t, up), has_up, has_down, tx_top, h_below),
        ((t, down), has_down, has_up, tx_bot, rest[0]),
        ((left, k), has_left, has_right, tx_left, h_right),
        ((right, k), has_right, has_left, tx_right, h_left),
        ((right, up), both(has_right, has_up), both(has_left, has_down), corner, rest[1]),
        ((left, up), both(has_left, has_up), both(has_right, has_down), corner, rest[2]),
        ((right, down), both(has_right, has_down), both(has_left, has_up), tx_bot, rest[3]),
        ((left, down), both(has_left, has_down), both(has_right, has_up), tx_bot, rest[4]),
    ]
    near_here = greet([(p[0], p[1]) for p in plan[2:]] + [(above, None), (below, None)])

    def tell(r):
        for side, target in enumerate((above, below)):
            pl.semaphore_signal(
                reach_sems.at[2 * r + side], inc=1, device_id=target, device_id_type=MESH
            )

    def told(r):
        for side in (0, 1):
            pl.semaphore_wait(reach_sems.at[2 * r + side], 1)

    halo = [
        (there, comes, remote(src, dst, halo_send.at[i], halo_recv.at[i], target))
        for i, (target, there, comes, src, dst) in enumerate(plan)
    ]
    for load in loads[:3]:
        load.wait()
    visc_c = load_slices(visc)
    fib = [load_slices(fibre, (c,)) for c in range(3)]
    v_c = [load_slices(vel, (c,)) for c in range(3)]
    fields = v_c + [visc_c]
    tx_bot[0] = pack_rows([f[0] for f in fields], 0)
    tx_top[0] = pack_rows([f[7] for f in fields], 3)
    tx_top[1] = pack_rows([f[7] for f in fib], 3)
    pack_sides(tx_left, tx_right, fields)
    near_here()
    for there, _, copy in halo:
        when(there, copy.start)
    for r in range(half - 2):
        tell(r)
        told(r)
    tell(half - 2)
    place = edges(tiles, groups)
    rows, low, side_ok, has_below, has_above = place
    pos = rows % 4
    inner = pos < 3
    loads[3].wait()
    loads[4].wait()
    mass_c = load_slices(mass)
    for _, comes, copy in halo[:2]:
        when(comes, copy.wait_recv)
    centre = (
        [below_slice(visc_c, h_below[0], 3, has_below, rows)]
        + visc_c
        + [above_slice(visc_c, h_rest[0], 3, has_above, rows)]
    )
    fib = [[below_slice(fib[c], h_below[1], c, has_below, rows)] + fib[c] for c in range(3)]
    face = []
    for v in range(SLICES + 1):
        mu = 0.5 * (centre[v] + centre[v + 1])
        f = [fib[c][v] for c in range(3)]
        g = [mu * q for q in f]
        face.append(
            [mu + g[0] * f[0], g[0] * f[1], g[0] * f[2], mu + g[1] * f[1], g[1] * f[2], mu + g[2] * f[2]]
        )
    diag, link = [], []
    for v in range(SLICES):
        d = plus(face[v], face[v + 1])
        m = mass_c[v] * centre[v + 1]
        for i in (0, 3, 5):
            d[i] = d[i] + m
        diag.append(d)
        link.append(full(face[v]))
    top_diag = diag[7]
    joined = jnp.logical_or(pos > 0, has_below)
    link[0] = [keep(joined, r) for r in link[0]]
    done = []
    low_d = None
    for step, e in ORDER:
        n, p = e + step, e - step
        solved, to_p, to_n, passed = eliminate(diag[e], link[e], link[n])
        done.append(solved)
        diag[n], link[n] = minus(diag[n], to_n), passed
        if p >= 0:
            diag[p] = minus(diag[p], to_p)
        else:
            low_d = to_p if low_d is None else plus(low_d, to_p)
    d7 = minus(diag[7], keep(inner, moved(low_d, -1)))
    done4, done5, base_d, last_d, last_l = reduce_matrix(d7, link[7], pos)
    out = moved(plus(base_d, low_d), 3) + last_d + [e for r in last_l for e in r]
    for i in range(6):
        matrix_own[i] = pack_rows(out[4 * i : 4 * i + 4], 3)
    mat_copies = [
        remote(matrix_own, matrix_all.at[k], mat_send.at[i], mat_recv.at[i], p)
        for i, p in enumerate(peers[1:])
    ]
    passed_up = matrix_all.at[lax.rem(k + groups - half + 1, groups), pl.ds(0, 3)]
    passed_down = matrix_all.at[lax.rem(k + half - 1, groups), pl.ds(3, 3)]
    relays = [
        remote(passed_up, passed_up, relay_send.at[0], relay_recv.at[0], above),
        remote(passed_down, passed_down, relay_send.at[1], relay_recv.at[1], below),
    ]
    told(half - 2)
    for copy in mat_copies:
        copy.start()
    matrix_all[k] = matrix_own[...]

    for _, comes, copy in halo[2:]:
        when(comes, copy.wait_recv)
    around = (h_left, h_right, h_below, h_rest, place)
    visc_ext = extended(visc_c, 3, *around)
    weight = stencil_weight(visc_ext)
    source = [[] for _ in range(SLICES)]
    for c in range(3):
        image = stencil(extended(v_c[c], c, *around), visc_ext, weight)
        force_c = load_slices(force, (c,))
        for v in range(SLICES):
            source[v].append(force_c[v] - image[v])
    top_source = source[7]
    ys = []
    low_s = None
    for (step, e), solved in zip(ORDER, done):
        n, p = e + step, e - step
        y, to_p, to_n = push(solved, source[e])
        ys.append(y)
        source[n] = plus(source[n], to_n)
        if p >= 0:
            source[p] = plus(source[p], to_p)
        else:
            low_s = to_p if low_s is None else plus(low_s, to_p)
    s7 = plus(source[7], keep(inner, moved(low_s, -1)))
    y4, y5, base_s, last_s = reduce_source(done4, done5, s7, pos)
    out = moved(plus(base_s, low_s), 3) + last_s
    source_own[0] = pack_rows(out[:4], 3)
    source_own[1] = pack_rows(out[4:], 3)
    src_copies = [
        remote(source_own, source_all.at[k], src_send.at[i], src_recv.at[i], p)
        for i, p in enumerate(peers)
    ]
    for copy in src_copies:
        copy.start()
    source_all[k] = source_own[...]
    for i in range(SLICES + 2):
        visc_out[i] = visc_ext[0][i]
        visc_out[SLICES + 2 + i] = visc_ext[1][i]
    for v in range(SLICES):
        visc_out[2 * SLICES + 4 + v] = weight[v]

    for copy, relay in zip(mat_copies[:2], relays):
        copy.wait_recv()
        relay.start()

    def gathered(ref, lo, hi, h):
        values = []
        for f in range(lo, hi):
            value = None
            for s in range(4):
                part = roll_rows(ref[2 * s + h, f // 4], s - f % 4)
                value = part if value is None else jnp.where(pos == s, part, value)
            values.append(value)
        return values

    def link_of(h):
        e = gathered(matrix_all, 12, 21, h)
        return [e[0:3], e[3:6], e[6:9]]

    for copy in mat_copies[2:] + relays:
        copy.wait_recv()
    d0 = minus(gathered(matrix_all, 6, 12, 0), gathered(matrix_all, 0, 6, 1))
    d1 = minus(
        gathered(matrix_all, 6, 12, 1), keep(inner, moved(gathered(matrix_all, 0, 6, 0), -1))
    )
    r_h, to_p, to_n, passed = eliminate(d0, link_of(0), link_of(1))
    d1 = minus(minus(d1, to_n), keep(inner, moved(to_p, -1)))
    r4, r5, _, end_d, _ = reduce_matrix(d1, passed, pos)
    end_inv = full(sym_inverse(end_d))
    face_inv = full(sym_inverse(face[8]))
    for copy in src_copies:
        copy.wait_recv()
    s0 = plus(gathered(source_all, 3, 6, 0), gathered(source_all, 0, 3, 1))
    s1 = plus(
        gathered(source_all, 3, 6, 1), keep(inner, moved(gathered(source_all, 0, 3, 0), -1))
    )
    z_h, to_p, to_n = push(r_h, s0)
    s1 = plus(plus(s1, to_n), keep(inner, moved(to_p, -1)))
    z4, z5, _, end_s = reduce_source(r4, r5, s1, pos)
    nothing = [jnp.zeros(TILE, jnp.float32)] * 3
    x1 = expand_rows(r4, r5, z4, z5, nothing, mat_vec(end_inv, end_s), pos)
    x0 = back(r_h, z_h, keep(pos > 0, moved(x1, 1)), x1)
    own, base = nothing, nothing
    for g in range(groups):
        x = (x0, x1)[g % 2]
        own = select(k == g, moved(x, 3 - g // 2), own)
        base = select(k == g + 1, moved(x, -(g // 2)), base)
    x = [None] * SLICES
    x[7] = expand_rows(done4, done5, y4, y5, base, own, pos)
    under = select(pos == 0, base, moved(x[7], 1))
    for (step, e), solved, y in reversed(list(zip(ORDER, done, ys))):
        x[e] = back(solved, y, under if e < step else x[e - step], x[e + step])
    rhs = minus(mat_vec(full(top_diag), x[7]), mat_vec(full(face[7]), x[6]))
    over = keep(has_above, mat_vec(face_inv, minus(rhs, top_source)))
    pack_sides(ux_left, ux_right, [[x[v][c] for v in range(SLICES)] for c in range(3)])
    packed_base, packed_over = pack_rows(base, 0), pack_rows(over, 3)
    ux_left[12] = jnp.where(low, packed_base, roll_rows(packed_over, 4))
    ux_right[12] = jnp.where(low, roll_rows(packed_base, 4), packed_over)
    last = [
        (has_left, has_right, remote(ux_left, rx_right, upd_send.at[0], upd_recv.at[0], (left, k))),
        (has_right, has_left, remote(ux_right, rx_left, upd_send.at[1], upd_recv.at[1], (right, k))),
    ]
    for there, _, copy in last:
        when(there, copy.start)
    for c in range(3):
        for v in range(SLICES):
            update[8 * c + v] = x[v][c]
        ends[c] = base[c]
        ends[3 + c] = over[c]
    for there, _, copy in halo:
        when(there, copy.wait_send)
    for copy in mat_copies + relays + src_copies:
        copy.wait_send()
    for there, comes, copy in last:
        when(comes, copy.wait_recv)
        when(there, copy.wait_send)


def image_kernel(
    tiles, groups, solved, ends, visc, rx_left, rx_right, update_out, image_out, update, image, sems
):
    for c in range(3):
        store_slices(update, (c,), [solved[8 * c + v] for v in range(SLICES)])
    copies = [pltpu.make_async_copy(update, update_out, sems.at[3])]
    copies[0].start()
    rows, low, side_ok, has_below, has_above = edges(tiles, groups)
    pos = rows % 4
    visc_ext = ([visc[i] for i in range(10)], [visc[10 + i] for i in range(10)])
    weight = [visc[20 + v] for v in range(SLICES)]
    for c in range(3):
        x = [solved[8 * c + v] for v in range(SLICES)]
        sides = []
        for m in range(4):
            lt, rt = rx_left[4 * c + m], rx_right[4 * c + m]
            sides.append(jnp.where(side_ok, jnp.where(low, lt, roll_rows(rt, 4)), 0.0))
            sides.append(jnp.where(side_ok, jnp.where(low, roll_rows(lt, 4), rt), 0.0))
        lt, rt = rx_left[12], rx_right[12]
        under = jnp.where(low, roll_rows(lt, -c), roll_rows(rt, 4 - c))
        over = jnp.where(low, roll_rows(lt, -1 - c), roll_rows(rt, 3 - c))
        centre = (
            [jnp.where(pos == 0, ends[c], roll_rows(x[7], 1))]
            + x
            + [jnp.where(pos == 3, ends[3 + c], roll_rows(x[0], -1))]
        )
        sides = (
            [jnp.where(pos == 0, jnp.where(side_ok, under, 0.0), roll_rows(sides[7], 1))]
            + sides
            + [jnp.where(pos == 3, jnp.where(side_ok, over, 0.0), roll_rows(sides[0], -1))]
        )
        store_slices(image, (c,), stencil((centre, sides), visc_ext, weight))
        copies.append(pltpu.make_async_copy(image.at[c], image_out.at[c], sems.at[c]))
        copies[-1].start()
    for copy in copies:
        copy.wait()


def tiles_of(*lead):
    return jax.ShapeDtypeStruct(lead + TILE, jnp.float32)


def per_device(tiles, groups, velocity, forcing, viscosity, fibre, inertia):
    vel, force, fib = (a.reshape(3, 64, 128) for a in (velocity, forcing, fibre))
    visc, mass = viscosity.reshape(64, 128), inertia.reshape(64, 128)
    bind = functools.partial
    vmem = pl.BlockSpec(memory_space=pltpu.VMEM)
    hbm = pl.BlockSpec(memory_space=pltpu.HBM)
    block = jax.ShapeDtypeStruct((3, 64, 128), jnp.float32)

    def space(*shape):
        return pltpu.VMEM(shape, jnp.float32)

    def tiles_in(*lead):
        return space(*lead, *TILE)

    dma = pltpu.SemaphoreType.DMA
    inputs = [pltpu.with_memory_space_constraint(a, pltpu.HBM) for a in (vel, force, visc, fib, mass)]
    parts = pl.pallas_call(
        bind(solve_kernel, tiles, groups),
        out_shape=[tiles_of(n) for n in (24, 6, 28, 13, 13)],
        in_specs=[hbm] * 5,
        out_specs=[vmem] * 5,
        scratch_shapes=[
            space(3, 64, 128), space(3, 64, 128), space(64, 128), space(3, 64, 128), space(64, 128),
            tiles_in(16), tiles_in(16), tiles_in(2), tiles_in(1),
            tiles_in(16), tiles_in(16), tiles_in(2), tiles_in(5),
            tiles_in(6), tiles_in(groups, 6), tiles_in(2), tiles_in(groups, 2),
            tiles_in(13), tiles_in(13),
            dma((5,)), dma((8,)), dma((8,)),
            dma((groups - 2,)), dma((groups - 2,)), dma((groups - 1,)), dma((groups - 1,)),
            dma((2,)), dma((2,)), dma((2,)), dma((2,)),
            pltpu.SemaphoreType.REGULAR((groups - 2,)),
        ],
        compiler_params=pltpu.CompilerParams(
            collective_id=0, has_side_effects=True, vmem_limit_bytes=16 * 1024 * 1024
        ),
        name="solve",
    )(*inputs)
    update, image = pl.pallas_call(
        bind(image_kernel, tiles, groups),
        out_shape=[block, block],
        in_specs=[vmem] * 5,
        out_specs=[hbm] * 2,
        scratch_shapes=[space(3, 64, 128), space(3, 64, 128), dma((4,))],
        compiler_params=pltpu.CompilerParams(vmem_limit_bytes=16 * 1024 * 1024),
        name="image",
    )(*parts)
    return update.reshape(velocity.shape), image.reshape(velocity.shape)


def solution(mesh):
    wide, flat = P(None, "thick", "tile", None), P("thick", "tile", None)
    return jax.shard_map(
        functools.partial(per_device, mesh.shape["tile"], mesh.shape["thick"]),
        mesh=mesh,
        in_specs=(wide, wide, flat, wide, flat),
        out_specs=(wide, wide),
        check_vma=False,
    )
```

```python
import functools

import jax
import jax.numpy as jnp
from jax import lax
from jax.experimental import pallas as pl
from jax.experimental.pallas import tpu as pltpu
from jax.sharding import PartitionSpec as P

MESH = pl.DeviceIdType.MESH
SLICES = 8
SYM = ((0, 1, 2), (1, 3, 4), (2, 4, 5))
TILE = (8, 128)


def roll_rows(values, shift):
    return values if shift % 8 == 0 else pltpu.roll(values, shift % 8, 0)


def row_ids():
    return lax.broadcasted_iota(jnp.int32, TILE, 0)


def load_slices(ref, lead=()):
    def one(v):
        halves = [ref[lead + (pl.ds(2 * v + x, 4, stride=16), slice(None))] for x in (0, 1)]
        return jnp.concatenate(halves, axis=0)

    return [one(v) for v in range(SLICES)]


def store_slices(ref, lead, slices):
    for v in range(SLICES):
        for x in (0, 1):
            ref[lead + (pl.ds(2 * v + x, 4, stride=16), slice(None))] = slices[v][4 * x : 4 * x + 4]


def pack_rows(fields, pos):
    rows = row_ids() % 4
    packed = roll_rows(fields[0], -pos)
    for j in range(1, len(fields)):
        packed = jnp.where(rows == j, roll_rows(fields[j], j - pos), packed)
    return packed


def pack_side(ref, side, fields):
    low = row_ids() < 4
    for j, slices in enumerate(fields):
        for m in range(4):
            first, second = slices[2 * m], slices[2 * m + 1]
            if side == 0:
                ref[4 * j + m] = jnp.where(low, first, roll_rows(second, 4))
            else:
                ref[4 * j + m] = jnp.where(low, roll_rows(first, 4), second)


def greet(targets):
    barrier = pltpu.get_barrier_semaphore()
    count = 0
    for target, there in targets:
        if there is None:
            pl.semaphore_signal(barrier, inc=1, device_id=target, device_id_type=MESH)
            count = count + 1
        else:

            @pl.when(there)
            def _():
                pl.semaphore_signal(barrier, inc=1, device_id=target, device_id_type=MESH)

            count = count + there.astype(jnp.int32)
    return lambda: pl.semaphore_wait(barrier, count)


def remote(src, dst, send_sem, recv_sem, target):
    return pltpu.make_async_remote_copy(
        src_ref=src, dst_ref=dst, send_sem=send_sem, recv_sem=recv_sem,
        device_id=target, device_id_type=MESH,
    )


def when(there, action):
    pl.when(there)(lambda: action())


def edges(tiles, groups):
    t, k = lax.axis_index("tile"), lax.axis_index("thick")
    rows = row_ids()
    low = rows < 4
    side_ok = jnp.logical_or(
        jnp.logical_and(low, t > 0), jnp.logical_and(jnp.logical_not(low), t < tiles - 1)
    )
    return rows, low, side_ok, k > 0, k < groups - 1


def below_slice(slices, packed, j, has_below, rows):
    inside = roll_rows(slices[7], 1)
    return jnp.where(rows % 4 == 0, jnp.where(has_below, roll_rows(packed, -j), 0.0), inside)


def above_slice(slices, packed, j, has_above, rows):
    inside = roll_rows(slices[0], -1)
    return jnp.where(rows % 4 == 3, jnp.where(has_above, roll_rows(packed, 3 - j), 0.0), inside)


def extended(slices, j, rx_left, rx_right, rx_below, rx_rest, place):
    rows, low, side_ok, has_below, has_above = place
    sides = []
    for m in range(4):
        left, right = rx_left[4 * j + m], rx_right[4 * j + m]
        sides.append(jnp.where(side_ok, jnp.where(low, left, roll_rows(right, 4)), 0.0))
        sides.append(jnp.where(side_ok, jnp.where(low, roll_rows(left, 4), right), 0.0))
    centre = (
        [below_slice(slices, rx_below[0], j, has_below, rows)]
        + slices
        + [above_slice(slices, rx_rest[0], j, has_above, rows)]
    )
    below = roll_rows(jnp.where(low, rx_rest[2], rx_rest[1]), 4 - j)
    above = roll_rows(jnp.where(low, rx_rest[4], rx_rest[3]), 7 - j)
    below = jnp.where(jnp.logical_and(side_ok, has_below), below, 0.0)
    above = jnp.where(jnp.logical_and(side_ok, has_above), above, 0.0)
    sides = (
        [jnp.where(rows % 4 == 0, below, roll_rows(sides[7], 1))]
        + sides
        + [jnp.where(rows % 4 == 3, above, roll_rows(sides[0], -1))]
    )
    return centre, sides


def smooth(centre, sides):
    lanes = lax.broadcasted_iota(jnp.int32, TILE, 1)
    across = [c + 0.5 * (roll_rows(c, 4) + s) for c, s in zip(centre, sides)]
    out = []
    for v in range(SLICES):
        z = across[v + 1] + 0.5 * (across[v] + across[v + 2])
        up = jnp.where(lanes < 127, pltpu.roll(z, 127, 1), 0.0)
        down = jnp.where(lanes > 0, pltpu.roll(z, 1, 1), 0.0)
        out.append(z + 0.5 * (up + down))
    return out


def stencil(field, visc, weight):
    centre, sides = field
    visc_centre, visc_sides = visc
    flat = smooth(centre, sides)
    scaled = smooth(
        [a * b for a, b in zip(visc_centre, centre)], [a * b for a, b in zip(visc_sides, sides)]
    )
    return [
        (1.0 / 3.0) * (centre[v + 1] * weight[v] - visc_centre[v + 1] * flat[v] - scaled[v])
        for v in range(SLICES)
    ]


def stencil_weight(visc):
    flat = smooth(*visc)
    return [8.0 * visc[0][v + 1] + flat[v] for v in range(SLICES)]


def sym_inverse(d):
    a, b, c, e, f, g = d
    c00, c01, c02 = e * g - f * f, c * f - b * g, b * f - c * e
    r = 1.0 / (a * c00 + b * c01 + c * c02)
    return [r * q for q in (c00, c01, c02, a * g - c * c, b * c - a * f, a * e - b * b)]


def dot3(xs, ys):
    return xs[0] * ys[0] + xs[1] * ys[1] + xs[2] * ys[2]


def mat_vec(m, x):
    return [dot3(m[i], x) for i in range(3)]


def mat_mat(m, n):
    return [[dot3(m[i], [n[0][j], n[1][j], n[2][j]]) for j in range(3)] for i in range(3)]


def sym_product(m, n):
    return [dot3(m[i], [n[0][j], n[1][j], n[2][j]]) for i in range(3) for j in range(i, 3)]


def transposed(m):
    return [[m[j][i] for j in range(3)] for i in range(3)]


def full(d):
    return [[d[SYM[i][j]] for j in range(3)] for i in range(3)]


def eliminate(diag, to_prev, next_to):
    inv = full(sym_inverse(diag))
    pm = mat_mat(inv, to_prev)
    qm = mat_mat(inv, transposed(next_to))
    to_p = sym_product(transposed(to_prev), pm)
    return (inv, pm, qm), to_p, sym_product(next_to, qm), mat_mat(next_to, pm)


def push(done, source):
    inv, pm, qm = done
    return mat_vec(inv, source), mat_vec(transposed(pm), source), mat_vec(transposed(qm), source)


def back(done, y, x_prev, x_next):
    _, pm, qm = done
    return [y[i] + dot3(pm[i], x_prev) + dot3(qm[i], x_next) for i in range(3)]


def minus(a, b):
    return [x - y for x, y in zip(a, b)]


def plus(a, b):
    return [x + y for x, y in zip(a, b)]


def select(mask, a, b):
    return [jnp.where(mask, x, y) for x, y in zip(a, b)]


def keep(mask, a):
    return [jnp.where(mask, x, 0.0) for x in a]


def moved(a, shift):
    return [roll_rows(x, shift) for x in a]


def moved_mat(m, shift):
    return [moved(r, shift) for r in m]


def reduce_matrix(diag, link, pos):
    done4, to_p, to_n, passed = eliminate(diag, link, moved_mat(link, -1))
    base = keep(pos == 0, to_p)
    diag = minus(diag, plus(moved(to_n, 1), keep(pos == 1, moved(to_p, -1))))
    link = moved_mat(passed, 1)
    done5, to_p, to_n, passed = eliminate(diag, link, moved_mat(link, -2))
    base = plus(base, keep(pos == 0, moved(to_p, -1)))
    return done4, done5, base, minus(diag, moved(to_n, 2)), moved_mat(passed, 2)


def reduce_source(done4, done5, source, pos):
    y4, to_p, to_n = push(done4, source)
    base = keep(pos == 0, to_p)
    source = plus(source, plus(moved(to_n, 1), keep(pos == 1, moved(to_p, -1))))
    y5, to_p, to_n = push(done5, source)
    base = plus(base, keep(pos == 0, moved(to_p, -1)))
    return y4, y5, base, plus(source, moved(to_n, 2))


def expand_rows(done4, done5, y4, y5, x_base, x_last, pos):
    x_one = back(done5, y5, moved(x_base, 1), moved(x_last, -2))
    kept = select(pos == 1, x_one, x_last)
    x_even = back(done4, y4, select(pos == 0, x_base, moved(kept, 1)), moved(kept, -1))
    return select(pos % 2 == 0, x_even, kept)


ORDER = ((1, 0), (1, 2), (1, 4), (1, 6), (2, 1), (2, 5), (4, 3))


def solve_kernel(
    tiles, groups, vel_in, force_in, visc_in, fibre_in, mass_in,
    update, ends, visc_out, rx_left, rx_right,
    vel, force, visc, fibre, mass, tx_left, tx_right, tx_top, tx_bot,
    h_left, h_right, h_below, h_rest, matrix_own, matrix_all, source_own, source_all,
    ux_left, ux_right, load_sems, halo_send, halo_recv, mat_send, mat_recv, src_send, src_recv,
    upd_send, upd_recv, relay_send, relay_recv, reach_sems,
):
    t, k = lax.axis_index("tile"), lax.axis_index("thick")
    loads = [
        pltpu.make_async_copy(src, dst, load_sems.at[i])
        for i, (src, dst) in enumerate(
            ((visc_in, visc), (fibre_in, fibre), (vel_in, vel), (mass_in, mass), (force_in, force))
        )
    ]
    for load in loads:
        load.start()
    has_left, has_right, has_down, has_up = t > 0, t < tiles - 1, k > 0, k < groups - 1
    left, right = jnp.maximum(t - 1, 0), jnp.minimum(t + 1, tiles - 1)
    down, up = jnp.maximum(k - 1, 0), jnp.minimum(k + 1, groups - 1)
    both = jnp.logical_and
    half = groups // 2
    ring = [d for j in range(half, 0, -1) for d in sorted({j, groups - j})]
    peers = [(t, lax.rem(k + d, groups)) for d in ring]
    above, below = (t, lax.rem(k + 1, groups)), (t, lax.rem(k + groups - 1, groups))
    corner = tx_top.at[pl.ds(0, 1)]
    rest = [h_rest.at[pl.ds(i, 1)] for i in range(5)]
    plan = [
        ((t, up), has_up, has_down, tx_top, h_below),
        ((t, down), has_down, has_up, tx_bot, rest[0]),
        ((right, up), both(has_right, has_up), both(has_left, has_down), corner, rest[1]),
        ((left, up), both(has_left, has_up), both(has_right, has_down), corner, rest[2]),
        ((right, down), both(has_right, has_down), both(has_left, has_up), tx_bot, rest[3]),
        ((left, down), both(has_left, has_down), both(has_right, has_up), tx_bot, rest[4]),
        ((left, k), has_left, has_right, tx_left, h_right),
        ((right, k), has_right, has_left, tx_right, h_left),
    ]
    near_here = greet([(p[0], p[1]) for p in plan[2:]] + [(above, None), (below, None)])

    def tell(r):
        for side, target in enumerate((above, below)):
            pl.semaphore_signal(
                reach_sems.at[2 * r + side], inc=1, device_id=target, device_id_type=MESH
            )

    def told(r):
        for side in (0, 1):
            pl.semaphore_wait(reach_sems.at[2 * r + side], 1)

    halo = [
        (there, comes, remote(src, dst, halo_send.at[i], halo_recv.at[i], target))
        for i, (target, there, comes, src, dst) in enumerate(plan)
    ]
    for load in loads[:3]:
        load.wait()
    visc_c = load_slices(visc)
    fib = [load_slices(fibre, (c,)) for c in range(3)]
    v_c = [load_slices(vel, (c,)) for c in range(3)]
    fields = v_c + [visc_c]
    tx_bot[0] = pack_rows([f[0] for f in fields], 0)
    tx_top[0] = pack_rows([f[7] for f in fields], 3)
    tx_top[1] = pack_rows([f[7] for f in fib], 3)
    near_here()
    for there, _, copy in halo[:6]:
        when(there, copy.start)
    for side, ref in enumerate((tx_left, tx_right)):
        pack_side(ref, side, fields)
        there, _, copy = halo[6 + side]
        when(there, copy.start)
    for r in range(half - 2):
        tell(r)
        told(r)
    tell(half - 2)
    place = edges(tiles, groups)
    rows, low, side_ok, has_below, has_above = place
    pos = rows % 4
    inner = pos < 3
    loads[3].wait()
    loads[4].wait()
    mass_c = load_slices(mass)
    for _, comes, copy in halo[:2]:
        when(comes, copy.wait_recv)
    centre = (
        [below_slice(visc_c, h_below[0], 3, has_below, rows)]
        + visc_c
        + [above_slice(visc_c, h_rest[0], 3, has_above, rows)]
    )
    fib = [[below_slice(fib[c], h_below[1], c, has_below, rows)] + fib[c] for c in range(3)]
    face = []
    for v in range(SLICES + 1):
        mu = 0.5 * (centre[v] + centre[v + 1])
        f = [fib[c][v] for c in range(3)]
        g = [mu * q for q in f]
        face.append(
            [mu + g[0] * f[0], g[0] * f[1], g[0] * f[2], mu + g[1] * f[1], g[1] * f[2], mu + g[2] * f[2]]
        )
    diag, link = [], []
    for v in range(SLICES):
        d = plus(face[v], face[v + 1])
        m = mass_c[v] * centre[v + 1]
        for i in (0, 3, 5):
            d[i] = d[i] + m
        diag.append(d)
        link.append(full(face[v]))
    top_diag = diag[7]
    joined = jnp.logical_or(pos > 0, has_below)
    link[0] = [keep(joined, r) for r in link[0]]
    done = []
    low_d = None
    for step, e in ORDER:
        n, p = e + step, e - step
        solved, to_p, to_n, passed = eliminate(diag[e], link[e], link[n])
        done.append(solved)
        diag[n], link[n] = minus(diag[n], to_n), passed
        if p >= 0:
            diag[p] = minus(diag[p], to_p)
        else:
            low_d = to_p if low_d is None else plus(low_d, to_p)
    d7 = minus(diag[7], keep(inner, moved(low_d, -1)))
    done4, done5, base_d, last_d, last_l = reduce_matrix(d7, link[7], pos)
    out = moved(plus(base_d, low_d), 3) + last_d + [e for r in last_l for e in r]
    for i in range(6):
        matrix_own[i] = pack_rows(out[4 * i : 4 * i + 4], 3)
    mat_copies = [
        remote(matrix_own, matrix_all.at[k], mat_send.at[i], mat_recv.at[i], p)
        for i, p in enumerate(peers[1:])
    ]
    passed_up = matrix_all.at[lax.rem(k + groups - half + 1, groups), pl.ds(0, 3)]
    passed_down = matrix_all.at[lax.rem(k + half - 1, groups), pl.ds(3, 3)]
    relays = [
        remote(passed_up, passed_up, relay_send.at[0], relay_recv.at[0], above),
        remote(passed_down, passed_down, relay_send.at[1], relay_recv.at[1], below),
    ]
    told(half - 2)
    for copy in mat_copies:
        copy.start()
    matrix_all[k] = matrix_own[...]

    for _, comes, copy in halo[2:]:
        when(comes, copy.wait_recv)
    around = (h_left, h_right, h_below, h_rest, place)
    visc_ext = extended(visc_c, 3, *around)
    weight = stencil_weight(visc_ext)
    source = [[] for _ in range(SLICES)]
    for c in range(3):
        image = stencil(extended(v_c[c], c, *around), visc_ext, weight)
        force_c = load_slices(force, (c,))
        for v in range(SLICES):
            source[v].append(force_c[v] - image[v])
    top_source = source[7]
    ys = []
    low_s = None
    for (step, e), solved in zip(ORDER, done):
        n, p = e + step, e - step
        y, to_p, to_n = push(solved, source[e])
        ys.append(y)
        source[n] = plus(source[n], to_n)
        if p >= 0:
            source[p] = plus(source[p], to_p)
        else:
            low_s = to_p if low_s is None else plus(low_s, to_p)
    s7 = plus(source[7], keep(inner, moved(low_s, -1)))
    y4, y5, base_s, last_s = reduce_source(done4, done5, s7, pos)
    out = moved(plus(base_s, low_s), 3) + last_s
    source_own[0] = pack_rows(out[:4], 3)
    source_own[1] = pack_rows(out[4:], 3)
    src_copies = [
        remote(source_own, source_all.at[k], src_send.at[i], src_recv.at[i], p)
        for i, p in enumerate(peers)
    ]
    for copy in src_copies:
        copy.start()
    source_all[k] = source_own[...]
    for i in range(SLICES + 2):
        visc_out[i] = visc_ext[0][i]
        visc_out[SLICES + 2 + i] = visc_ext[1][i]
    for v in range(SLICES):
        visc_out[2 * SLICES + 4 + v] = weight[v]

    for copy, relay in zip(mat_copies[:2], relays):
        copy.wait_recv()
        relay.start()

    def gathered(ref, lo, hi, h):
        values = []
        for f in range(lo, hi):
            value = None
            for s in range(4):
                part = roll_rows(ref[2 * s + h, f // 4], s - f % 4)
                value = part if value is None else jnp.where(pos == s, part, value)
            values.append(value)
        return values

    def link_of(h):
        e = gathered(matrix_all, 12, 21, h)
        return [e[0:3], e[3:6], e[6:9]]

    for copy in mat_copies[2:] + relays:
        copy.wait_recv()
    d0 = minus(gathered(matrix_all, 6, 12, 0), gathered(matrix_all, 0, 6, 1))
    d1 = minus(
        gathered(matrix_all, 6, 12, 1), keep(inner, moved(gathered(matrix_all, 0, 6, 0), -1))
    )
    r_h, to_p, to_n, passed = eliminate(d0, link_of(0), link_of(1))
    d1 = minus(minus(d1, to_n), keep(inner, moved(to_p, -1)))
    r4, r5, _, end_d, _ = reduce_matrix(d1, passed, pos)
    end_inv = full(sym_inverse(end_d))
    face_inv = full(sym_inverse(face[8]))
    for copy in src_copies:
        copy.wait_recv()
    s0 = plus(gathered(source_all, 3, 6, 0), gathered(source_all, 0, 3, 1))
    s1 = plus(
        gathered(source_all, 3, 6, 1), keep(inner, moved(gathered(source_all, 0, 3, 0), -1))
    )
    z_h, to_p, to_n = push(r_h, s0)
    s1 = plus(plus(s1, to_n), keep(inner, moved(to_p, -1)))
    z4, z5, _, end_s = reduce_source(r4, r5, s1, pos)
    nothing = [jnp.zeros(TILE, jnp.float32)] * 3
    x1 = expand_rows(r4, r5, z4, z5, nothing, mat_vec(end_inv, end_s), pos)
    x0 = back(r_h, z_h, keep(pos > 0, moved(x1, 1)), x1)
    own, base = nothing, nothing
    for g in range(groups):
        x = (x0, x1)[g % 2]
        own = select(k == g, moved(x, 3 - g // 2), own)
        base = select(k == g + 1, moved(x, -(g // 2)), base)
    x = [None] * SLICES
    x[7] = expand_rows(done4, done5, y4, y5, base, own, pos)
    under = select(pos == 0, base, moved(x[7], 1))
    for (step, e), solved, y in reversed(list(zip(ORDER, done, ys))):
        x[e] = back(solved, y, under if e < step else x[e - step], x[e + step])
    rhs = minus(mat_vec(full(top_diag), x[7]), mat_vec(full(face[7]), x[6]))
    over = keep(has_above, mat_vec(face_inv, minus(rhs, top_source)))
    packed_base, packed_over = pack_rows(base, 0), pack_rows(over, 3)
    ux_left[12] = jnp.where(low, packed_base, roll_rows(packed_over, 4))
    ux_right[12] = jnp.where(low, roll_rows(packed_base, 4), packed_over)
    last = [
        (has_left, has_right, remote(ux_left, rx_right, upd_send.at[0], upd_recv.at[0], (left, k))),
        (has_right, has_left, remote(ux_right, rx_left, upd_send.at[1], upd_recv.at[1], (right, k))),
    ]
    fields = [[x[v][c] for v in range(SLICES)] for c in range(3)]
    for side, ref in enumerate((ux_left, ux_right)):
        pack_side(ref, side, fields)
        there, _, copy = last[side]
        when(there, copy.start)
    for c in range(3):
        for v in range(SLICES):
            update[8 * c + v] = x[v][c]
        ends[c] = base[c]
        ends[3 + c] = over[c]
    for there, _, copy in halo:
        when(there, copy.wait_send)
    for copy in mat_copies + relays + src_copies:
        copy.wait_send()
    for there, comes, copy in last:
        when(comes, copy.wait_recv)
        when(there, copy.wait_send)


def image_kernel(
    tiles, groups, solved, ends, visc, rx_left, rx_right, update_out, image_out, update, image, sems
):
    for c in range(3):
        store_slices(update, (c,), [solved[8 * c + v] for v in range(SLICES)])
    copies = [pltpu.make_async_copy(update, update_out, sems.at[3])]
    copies[0].start()
    rows, low, side_ok, has_below, has_above = edges(tiles, groups)
    pos = rows % 4
    visc_ext = ([visc[i] for i in range(10)], [visc[10 + i] for i in range(10)])
    weight = [visc[20 + v] for v in range(SLICES)]
    for c in range(3):
        x = [solved[8 * c + v] for v in range(SLICES)]
        sides = []
        for m in range(4):
            lt, rt = rx_left[4 * c + m], rx_right[4 * c + m]
            sides.append(jnp.where(side_ok, jnp.where(low, lt, roll_rows(rt, 4)), 0.0))
            sides.append(jnp.where(side_ok, jnp.where(low, roll_rows(lt, 4), rt), 0.0))
        lt, rt = rx_left[12], rx_right[12]
        under = jnp.where(low, roll_rows(lt, -c), roll_rows(rt, 4 - c))
        over = jnp.where(low, roll_rows(lt, -1 - c), roll_rows(rt, 3 - c))
        centre = (
            [jnp.where(pos == 0, ends[c], roll_rows(x[7], 1))]
            + x
            + [jnp.where(pos == 3, ends[3 + c], roll_rows(x[0], -1))]
        )
        sides = (
            [jnp.where(pos == 0, jnp.where(side_ok, under, 0.0), roll_rows(sides[7], 1))]
            + sides
            + [jnp.where(pos == 3, jnp.where(side_ok, over, 0.0), roll_rows(sides[0], -1))]
        )
        store_slices(image, (c,), stencil((centre, sides), visc_ext, weight))
        copies.append(pltpu.make_async_copy(image.at[c], image_out.at[c], sems.at[c]))
        copies[-1].start()
    for copy in copies:
        copy.wait()


def tiles_of(*lead):
    return jax.ShapeDtypeStruct(lead + TILE, jnp.float32)


def per_device(tiles, groups, velocity, forcing, viscosity, fibre, inertia):
    vel, force, fib = (a.reshape(3, 64, 128) for a in (velocity, forcing, fibre))
    visc, mass = viscosity.reshape(64, 128), inertia.reshape(64, 128)
    bind = functools.partial
    vmem = pl.BlockSpec(memory_space=pltpu.VMEM)
    hbm = pl.BlockSpec(memory_space=pltpu.HBM)
    block = jax.ShapeDtypeStruct((3, 64, 128), jnp.float32)

    def space(*shape):
        return pltpu.VMEM(shape, jnp.float32)

    def tiles_in(*lead):
        return space(*lead, *TILE)

    dma = pltpu.SemaphoreType.DMA
    inputs = [pltpu.with_memory_space_constraint(a, pltpu.HBM) for a in (vel, force, visc, fib, mass)]
    parts = pl.pallas_call(
        bind(solve_kernel, tiles, groups),
        out_shape=[tiles_of(n) for n in (24, 6, 28, 13, 13)],
        in_specs=[hbm] * 5,
        out_specs=[vmem] * 5,
        scratch_shapes=[
            space(3, 64, 128), space(3, 64, 128), space(64, 128), space(3, 64, 128), space(64, 128),
            tiles_in(16), tiles_in(16), tiles_in(2), tiles_in(1),
            tiles_in(16), tiles_in(16), tiles_in(2), tiles_in(5),
            tiles_in(6), tiles_in(groups, 6), tiles_in(2), tiles_in(groups, 2),
            tiles_in(13), tiles_in(13),
            dma((5,)), dma((8,)), dma((8,)),
            dma((groups - 2,)), dma((groups - 2,)), dma((groups - 1,)), dma((groups - 1,)),
            dma((2,)), dma((2,)), dma((2,)), dma((2,)),
            pltpu.SemaphoreType.REGULAR((groups - 2,)),
        ],
        compiler_params=pltpu.CompilerParams(
            collective_id=0, has_side_effects=True, vmem_limit_bytes=16 * 1024 * 1024
        ),
        name="solve",
    )(*inputs)
    update, image = pl.pallas_call(
        bind(image_kernel, tiles, groups),
        out_shape=[block, block],
        in_specs=[vmem] * 5,
        out_specs=[hbm] * 2,
        scratch_shapes=[space(3, 64, 128), space(3, 64, 128), dma((4,))],
        compiler_params=pltpu.CompilerParams(vmem_limit_bytes=16 * 1024 * 1024),
        name="image",
    )(*parts)
    return update.reshape(velocity.shape), image.reshape(velocity.shape)


def solution(mesh):
    wide, flat = P(None, "thick", "tile", None), P("thick", "tile", None)
    return jax.shard_map(
        functools.partial(per_device, mesh.shape["tile"], mesh.shape["thick"]),
        mesh=mesh,
        in_specs=(wide, wide, flat, wide, flat),
        out_specs=(wide, wide),
        check_vma=False,
    )
```

```python
import functools

import jax
import jax.numpy as jnp
from jax import lax
from jax.experimental import pallas as pl
from jax.experimental.pallas import tpu as pltpu
from jax.sharding import PartitionSpec as P

MESH = pl.DeviceIdType.MESH
SLICES = 8
SYM = ((0, 1, 2), (1, 3, 4), (2, 4, 5))
TILE = (8, 128)


def roll_rows(values, shift):
    return values if shift % 8 == 0 else pltpu.roll(values, shift % 8, 0)


def row_ids():
    return lax.broadcasted_iota(jnp.int32, TILE, 0)


def load_slices(ref, lead=()):
    def one(v):
        halves = [ref[lead + (pl.ds(2 * v + x, 4, stride=16), slice(None))] for x in (0, 1)]
        return jnp.concatenate(halves, axis=0)

    return [one(v) for v in range(SLICES)]


def store_slices(ref, lead, slices):
    for v in range(SLICES):
        for x in (0, 1):
            ref[lead + (pl.ds(2 * v + x, 4, stride=16), slice(None))] = slices[v][4 * x : 4 * x + 4]


def pack_rows(fields, pos):
    rows = row_ids() % 4
    packed = roll_rows(fields[0], -pos)
    for j in range(1, len(fields)):
        packed = jnp.where(rows == j, roll_rows(fields[j], j - pos), packed)
    return packed


def pack_side(ref, side, fields):
    low = row_ids() < 4
    for j, slices in enumerate(fields):
        for m in range(4):
            first, second = slices[2 * m], slices[2 * m + 1]
            if side == 0:
                ref[4 * j + m] = jnp.where(low, first, roll_rows(second, 4))
            else:
                ref[4 * j + m] = jnp.where(low, roll_rows(first, 4), second)


def greet(targets):
    barrier = pltpu.get_barrier_semaphore()
    count = 0
    for target, there in targets:
        if there is None:
            pl.semaphore_signal(barrier, inc=1, device_id=target, device_id_type=MESH)
            count = count + 1
        else:

            @pl.when(there)
            def _():
                pl.semaphore_signal(barrier, inc=1, device_id=target, device_id_type=MESH)

            count = count + there.astype(jnp.int32)
    return lambda: pl.semaphore_wait(barrier, count)


def remote(src, dst, send_sem, recv_sem, target):
    return pltpu.make_async_remote_copy(
        src_ref=src, dst_ref=dst, send_sem=send_sem, recv_sem=recv_sem,
        device_id=target, device_id_type=MESH,
    )


def when(there, action):
    pl.when(there)(lambda: action())


def edges(tiles, groups):
    t, k = lax.axis_index("tile"), lax.axis_index("thick")
    rows = row_ids()
    low = rows < 4
    side_ok = jnp.logical_or(
        jnp.logical_and(low, t > 0), jnp.logical_and(jnp.logical_not(low), t < tiles - 1)
    )
    return rows, low, side_ok, k > 0, k < groups - 1


def below_slice(slices, packed, j, has_below, rows):
    inside = roll_rows(slices[7], 1)
    return jnp.where(rows % 4 == 0, jnp.where(has_below, roll_rows(packed, -j), 0.0), inside)


def above_slice(slices, packed, j, has_above, rows):
    inside = roll_rows(slices[0], -1)
    return jnp.where(rows % 4 == 3, jnp.where(has_above, roll_rows(packed, 3 - j), 0.0), inside)


def extended(slices, j, rx_left, rx_right, rx_below, rx_rest, place):
    rows, low, side_ok, has_below, has_above = place
    sides = []
    for m in range(4):
        left, right = rx_left[4 * j + m], rx_right[4 * j + m]
        sides.append(jnp.where(side_ok, jnp.where(low, left, roll_rows(right, 4)), 0.0))
        sides.append(jnp.where(side_ok, jnp.where(low, roll_rows(left, 4), right), 0.0))
    centre = (
        [below_slice(slices, rx_below[0], j, has_below, rows)]
        + slices
        + [above_slice(slices, rx_rest[0], j, has_above, rows)]
    )
    below = roll_rows(jnp.where(low, rx_rest[2], rx_rest[1]), 4 - j)
    above = roll_rows(jnp.where(low, rx_rest[4], rx_rest[3]), 7 - j)
    below = jnp.where(jnp.logical_and(side_ok, has_below), below, 0.0)
    above = jnp.where(jnp.logical_and(side_ok, has_above), above, 0.0)
    sides = (
        [jnp.where(rows % 4 == 0, below, roll_rows(sides[7], 1))]
        + sides
        + [jnp.where(rows % 4 == 3, above, roll_rows(sides[0], -1))]
    )
    return centre, sides


def smooth(centre, sides):
    lanes = lax.broadcasted_iota(jnp.int32, TILE, 1)
    across = [c + 0.5 * (roll_rows(c, 4) + s) for c, s in zip(centre, sides)]
    out = []
    for v in range(SLICES):
        z = across[v + 1] + 0.5 * (across[v] + across[v + 2])
        up = jnp.where(lanes < 127, pltpu.roll(z, 127, 1), 0.0)
        down = jnp.where(lanes > 0, pltpu.roll(z, 1, 1), 0.0)
        out.append(z + 0.5 * (up + down))
    return out


def stencil(field, visc, weight):
    centre, sides = field
    visc_centre, visc_sides = visc
    flat = smooth(centre, sides)
    scaled = smooth(
        [a * b for a, b in zip(visc_centre, centre)], [a * b for a, b in zip(visc_sides, sides)]
    )
    return [
        (1.0 / 3.0) * (centre[v + 1] * weight[v] - visc_centre[v + 1] * flat[v] - scaled[v])
        for v in range(SLICES)
    ]


def stencil_weight(visc):
    flat = smooth(*visc)
    return [8.0 * visc[0][v + 1] + flat[v] for v in range(SLICES)]


def sym_inverse(d):
    a, b, c, e, f, g = d
    c00, c01, c02 = e * g - f * f, c * f - b * g, b * f - c * e
    r = 1.0 / (a * c00 + b * c01 + c * c02)
    return [r * q for q in (c00, c01, c02, a * g - c * c, b * c - a * f, a * e - b * b)]


def dot3(xs, ys):
    return xs[0] * ys[0] + xs[1] * ys[1] + xs[2] * ys[2]


def mat_vec(m, x):
    return [dot3(m[i], x) for i in range(3)]


def mat_mat(m, n):
    return [[dot3(m[i], [n[0][j], n[1][j], n[2][j]]) for j in range(3)] for i in range(3)]


def sym_product(m, n):
    return [dot3(m[i], [n[0][j], n[1][j], n[2][j]]) for i in range(3) for j in range(i, 3)]


def transposed(m):
    return [[m[j][i] for j in range(3)] for i in range(3)]


def full(d):
    return [[d[SYM[i][j]] for j in range(3)] for i in range(3)]


def eliminate(diag, to_prev, next_to):
    inv = full(sym_inverse(diag))
    pm = mat_mat(inv, to_prev)
    qm = mat_mat(inv, transposed(next_to))
    to_p = sym_product(transposed(to_prev), pm)
    return (inv, pm, qm), to_p, sym_product(next_to, qm), mat_mat(next_to, pm)


def push(done, source):
    inv, pm, qm = done
    return mat_vec(inv, source), mat_vec(transposed(pm), source), mat_vec(transposed(qm), source)


def back(done, y, x_prev, x_next):
    _, pm, qm = done
    return [y[i] + dot3(pm[i], x_prev) + dot3(qm[i], x_next) for i in range(3)]


def minus(a, b):
    return [x - y for x, y in zip(a, b)]


def plus(a, b):
    return [x + y for x, y in zip(a, b)]


def select(mask, a, b):
    return [jnp.where(mask, x, y) for x, y in zip(a, b)]


def keep(mask, a):
    return [jnp.where(mask, x, 0.0) for x in a]


def moved(a, shift):
    return [roll_rows(x, shift) for x in a]


def moved_mat(m, shift):
    return [moved(r, shift) for r in m]


def reduce_matrix(diag, link, pos):
    done4, to_p, to_n, passed = eliminate(diag, link, moved_mat(link, -1))
    base = keep(pos == 0, to_p)
    diag = minus(diag, plus(moved(to_n, 1), keep(pos == 1, moved(to_p, -1))))
    link = moved_mat(passed, 1)
    done5, to_p, to_n, passed = eliminate(diag, link, moved_mat(link, -2))
    base = plus(base, keep(pos == 0, moved(to_p, -1)))
    return done4, done5, base, minus(diag, moved(to_n, 2)), moved_mat(passed, 2)


def reduce_source(done4, done5, source, pos):
    y4, to_p, to_n = push(done4, source)
    base = keep(pos == 0, to_p)
    source = plus(source, plus(moved(to_n, 1), keep(pos == 1, moved(to_p, -1))))
    y5, to_p, to_n = push(done5, source)
    base = plus(base, keep(pos == 0, moved(to_p, -1)))
    return y4, y5, base, plus(source, moved(to_n, 2))


def expand_rows(done4, done5, y4, y5, x_base, x_last, pos):
    x_one = back(done5, y5, moved(x_base, 1), moved(x_last, -2))
    kept = select(pos == 1, x_one, x_last)
    x_even = back(done4, y4, select(pos == 0, x_base, moved(kept, 1)), moved(kept, -1))
    return select(pos % 2 == 0, x_even, kept)


ORDER = ((1, 0), (1, 2), (1, 4), (1, 6), (2, 1), (2, 5), (4, 3))


def solve_kernel(
    tiles, groups, vel_in, force_in, visc_in, fibre_in, mass_in,
    update, ends, visc_out, rx_left, rx_right,
    vel, force, visc, fibre, mass, tx_left, tx_right, tx_top, tx_bot,
    h_left, h_right, h_below, h_rest, matrix_own, matrix_all, source_own, source_all,
    ux_left, ux_right, load_sems, halo_send, halo_recv, mat_send, mat_recv, src_send, src_recv,
    upd_send, upd_recv, relay_send, relay_recv, reach_sems,
):
    t, k = lax.axis_index("tile"), lax.axis_index("thick")
    loads = [
        pltpu.make_async_copy(src, dst, load_sems.at[i])
        for i, (src, dst) in enumerate(
            ((visc_in, visc), (fibre_in, fibre), (vel_in, vel), (mass_in, mass), (force_in, force))
        )
    ]
    for load in loads:
        load.start()
    has_left, has_right, has_down, has_up = t > 0, t < tiles - 1, k > 0, k < groups - 1
    left, right = jnp.maximum(t - 1, 0), jnp.minimum(t + 1, tiles - 1)
    down, up = jnp.maximum(k - 1, 0), jnp.minimum(k + 1, groups - 1)
    both = jnp.logical_and
    half = groups // 2
    ring = [d for j in range(half, 0, -1) for d in sorted({j, groups - j})]
    peers = [(t, lax.rem(k + d, groups)) for d in ring]
    above, below = (t, lax.rem(k + 1, groups)), (t, lax.rem(k + groups - 1, groups))
    corner = tx_top.at[pl.ds(0, 1)]
    rest = [h_rest.at[pl.ds(i, 1)] for i in range(5)]
    plan = [
        ((t, up), has_up, has_down, tx_top, h_below),
        ((t, down), has_down, has_up, tx_bot, rest[0]),
        ((right, up), both(has_right, has_up), both(has_left, has_down), corner, rest[1]),
        ((left, up), both(has_left, has_up), both(has_right, has_down), corner, rest[2]),
        ((right, down), both(has_right, has_down), both(has_left, has_up), tx_bot, rest[3]),
        ((left, down), both(has_left, has_down), both(has_right, has_up), tx_bot, rest[4]),
    ]
    for j in (3, 0, 1, 2):
        part = pl.ds(4 * j, 4)
        plan.append(((left, k), has_left, has_right, tx_left.at[part], h_right.at[part]))
        plan.append(((right, k), has_right, has_left, tx_right.at[part], h_left.at[part]))
    near_here = greet([(p[0], p[1]) for p in plan[2:8]] + [(above, None), (below, None)])

    def tell(r):
        for side, target in enumerate((above, below)):
            pl.semaphore_signal(
                reach_sems.at[2 * r + side], inc=1, device_id=target, device_id_type=MESH
            )

    def told(r):
        for side in (0, 1):
            pl.semaphore_wait(reach_sems.at[2 * r + side], 1)

    halo = [
        (there, comes, remote(src, dst, halo_send.at[i], halo_recv.at[i], target))
        for i, (target, there, comes, src, dst) in enumerate(plan)
    ]
    for load in loads[:3]:
        load.wait()
    visc_c = load_slices(visc)
    fib = [load_slices(fibre, (c,)) for c in range(3)]
    v_c = [load_slices(vel, (c,)) for c in range(3)]
    fields = v_c + [visc_c]
    tx_bot[0] = pack_rows([f[0] for f in fields], 0)
    tx_top[0] = pack_rows([f[7] for f in fields], 3)
    tx_top[1] = pack_rows([f[7] for f in fib], 3)
    near_here()
    for there, _, copy in halo[:6]:
        when(there, copy.start)
    for i, j in enumerate((3, 0, 1, 2)):
        for side, ref in enumerate((tx_left, tx_right)):
            pack_side(ref.at[pl.ds(4 * j, 4)], side, [fields[j]])
            there, _, copy = halo[6 + 2 * i + side]
            when(there, copy.start)
    for r in range(half - 2):
        tell(r)
        told(r)
    tell(half - 2)
    place = edges(tiles, groups)
    rows, low, side_ok, has_below, has_above = place
    pos = rows % 4
    inner = pos < 3
    loads[3].wait()
    loads[4].wait()
    mass_c = load_slices(mass)
    for _, comes, copy in halo[:2]:
        when(comes, copy.wait_recv)
    centre = (
        [below_slice(visc_c, h_below[0], 3, has_below, rows)]
        + visc_c
        + [above_slice(visc_c, h_rest[0], 3, has_above, rows)]
    )
    fib = [[below_slice(fib[c], h_below[1], c, has_below, rows)] + fib[c] for c in range(3)]
    face = []
    for v in range(SLICES + 1):
        mu = 0.5 * (centre[v] + centre[v + 1])
        f = [fib[c][v] for c in range(3)]
        g = [mu * q for q in f]
        face.append(
            [mu + g[0] * f[0], g[0] * f[1], g[0] * f[2], mu + g[1] * f[1], g[1] * f[2], mu + g[2] * f[2]]
        )
    diag, link = [], []
    for v in range(SLICES):
        d = plus(face[v], face[v + 1])
        m = mass_c[v] * centre[v + 1]
        for i in (0, 3, 5):
            d[i] = d[i] + m
        diag.append(d)
        link.append(full(face[v]))
    top_diag = diag[7]
    joined = jnp.logical_or(pos > 0, has_below)
    link[0] = [keep(joined, r) for r in link[0]]
    done = []
    low_d = None
    for step, e in ORDER:
        n, p = e + step, e - step
        solved, to_p, to_n, passed = eliminate(diag[e], link[e], link[n])
        done.append(solved)
        diag[n], link[n] = minus(diag[n], to_n), passed
        if p >= 0:
            diag[p] = minus(diag[p], to_p)
        else:
            low_d = to_p if low_d is None else plus(low_d, to_p)
    d7 = minus(diag[7], keep(inner, moved(low_d, -1)))
    done4, done5, base_d, last_d, last_l = reduce_matrix(d7, link[7], pos)
    out = moved(plus(base_d, low_d), 3) + last_d + [e for r in last_l for e in r]
    for i in range(6):
        matrix_own[i] = pack_rows(out[4 * i : 4 * i + 4], 3)
    mat_copies = [
        remote(matrix_own, matrix_all.at[k], mat_send.at[i], mat_recv.at[i], p)
        for i, p in enumerate(peers[1:])
    ]
    passed_up = matrix_all.at[lax.rem(k + groups - half + 1, groups), pl.ds(0, 3)]
    passed_down = matrix_all.at[lax.rem(k + half - 1, groups), pl.ds(3, 3)]
    relays = [
        remote(passed_up, passed_up, relay_send.at[0], relay_recv.at[0], above),
        remote(passed_down, passed_down, relay_send.at[1], relay_recv.at[1], below),
    ]
    told(half - 2)
    for copy in mat_copies:
        copy.start()
    matrix_all[k] = matrix_own[...]

    for _, comes, copy in halo[2:8]:
        when(comes, copy.wait_recv)
    around = (h_left, h_right, h_below, h_rest, place)
    visc_ext = extended(visc_c, 3, *around)
    weight = stencil_weight(visc_ext)
    source = [[] for _ in range(SLICES)]
    for c in range(3):
        for _, comes, copy in halo[8 + 2 * c : 10 + 2 * c]:
            when(comes, copy.wait_recv)
        image = stencil(extended(v_c[c], c, *around), visc_ext, weight)
        force_c = load_slices(force, (c,))
        for v in range(SLICES):
            source[v].append(force_c[v] - image[v])
    top_source = source[7]
    ys = []
    low_s = None
    for (step, e), solved in zip(ORDER, done):
        n, p = e + step, e - step
        y, to_p, to_n = push(solved, source[e])
        ys.append(y)
        source[n] = plus(source[n], to_n)
        if p >= 0:
            source[p] = plus(source[p], to_p)
        else:
            low_s = to_p if low_s is None else plus(low_s, to_p)
    s7 = plus(source[7], keep(inner, moved(low_s, -1)))
    y4, y5, base_s, last_s = reduce_source(done4, done5, s7, pos)
    out = moved(plus(base_s, low_s), 3) + last_s
    source_own[0] = pack_rows(out[:4], 3)
    source_own[1] = pack_rows(out[4:], 3)
    src_copies = [
        remote(source_own, source_all.at[k], src_send.at[i], src_recv.at[i], p)
        for i, p in enumerate(peers)
    ]
    for copy in src_copies:
        copy.start()
    source_all[k] = source_own[...]
    for i in range(SLICES + 2):
        visc_out[i] = visc_ext[0][i]
        visc_out[SLICES + 2 + i] = visc_ext[1][i]
    for v in range(SLICES):
        visc_out[2 * SLICES + 4 + v] = weight[v]

    for copy, relay in zip(mat_copies[:2], relays):
        copy.wait_recv()
        relay.start()

    def gathered(ref, lo, hi, h):
        values = []
        for f in range(lo, hi):
            value = None
            for s in range(4):
                part = roll_rows(ref[2 * s + h, f // 4], s - f % 4)
                value = part if value is None else jnp.where(pos == s, part, value)
            values.append(value)
        return values

    def link_of(h):
        e = gathered(matrix_all, 12, 21, h)
        return [e[0:3], e[3:6], e[6:9]]

    for copy in mat_copies[2:] + relays:
        copy.wait_recv()
    d0 = minus(gathered(matrix_all, 6, 12, 0), gathered(matrix_all, 0, 6, 1))
    d1 = minus(
        gathered(matrix_all, 6, 12, 1), keep(inner, moved(gathered(matrix_all, 0, 6, 0), -1))
    )
    r_h, to_p, to_n, passed = eliminate(d0, link_of(0), link_of(1))
    d1 = minus(minus(d1, to_n), keep(inner, moved(to_p, -1)))
    r4, r5, _, end_d, _ = reduce_matrix(d1, passed, pos)
    end_inv = full(sym_inverse(end_d))
    face_inv = full(sym_inverse(face[8]))
    for copy in src_copies:
        copy.wait_recv()
    s0 = plus(gathered(source_all, 3, 6, 0), gathered(source_all, 0, 3, 1))
    s1 = plus(
        gathered(source_all, 3, 6, 1), keep(inner, moved(gathered(source_all, 0, 3, 0), -1))
    )
    z_h, to_p, to_n = push(r_h, s0)
    s1 = plus(plus(s1, to_n), keep(inner, moved(to_p, -1)))
    z4, z5, _, end_s = reduce_source(r4, r5, s1, pos)
    nothing = [jnp.zeros(TILE, jnp.float32)] * 3
    x1 = expand_rows(r4, r5, z4, z5, nothing, mat_vec(end_inv, end_s), pos)
    x0 = back(r_h, z_h, keep(pos > 0, moved(x1, 1)), x1)
    own, base = nothing, nothing
    for g in range(groups):
        x = (x0, x1)[g % 2]
        own = select(k == g, moved(x, 3 - g // 2), own)
        base = select(k == g + 1, moved(x, -(g // 2)), base)
    x = [None] * SLICES
    x[7] = expand_rows(done4, done5, y4, y5, base, own, pos)
    under = select(pos == 0, base, moved(x[7], 1))
    for (step, e), solved, y in reversed(list(zip(ORDER, done, ys))):
        x[e] = back(solved, y, under if e < step else x[e - step], x[e + step])
    rhs = minus(mat_vec(full(top_diag), x[7]), mat_vec(full(face[7]), x[6]))
    over = keep(has_above, mat_vec(face_inv, minus(rhs, top_source)))
    packed_base, packed_over = pack_rows(base, 0), pack_rows(over, 3)
    ux_left[12] = jnp.where(low, packed_base, roll_rows(packed_over, 4))
    ux_right[12] = jnp.where(low, roll_rows(packed_base, 4), packed_over)
    last = [
        (has_left, has_right, remote(ux_left, rx_right, upd_send.at[0], upd_recv.at[0], (left, k))),
        (has_right, has_left, remote(ux_right, rx_left, upd_send.at[1], upd_recv.at[1], (right, k))),
    ]
    fields = [[x[v][c] for v in range(SLICES)] for c in range(3)]
    for side, ref in enumerate((ux_left, ux_right)):
        pack_side(ref, side, fields)
        there, _, copy = last[side]
        when(there, copy.start)
    for c in range(3):
        for v in range(SLICES):
            update[8 * c + v] = x[v][c]
        ends[c] = base[c]
        ends[3 + c] = over[c]
    for there, _, copy in halo:
        when(there, copy.wait_send)
    for copy in mat_copies + relays + src_copies:
        copy.wait_send()
    for there, comes, copy in last:
        when(comes, copy.wait_recv)
        when(there, copy.wait_send)


def image_kernel(
    tiles, groups, solved, ends, visc, rx_left, rx_right, update_out, image_out, update, image, sems
):
    for c in range(3):
        store_slices(update, (c,), [solved[8 * c + v] for v in range(SLICES)])
    copies = [pltpu.make_async_copy(update, update_out, sems.at[3])]
    copies[0].start()
    rows, low, side_ok, has_below, has_above = edges(tiles, groups)
    pos = rows % 4
    visc_ext = ([visc[i] for i in range(10)], [visc[10 + i] for i in range(10)])
    weight = [visc[20 + v] for v in range(SLICES)]
    for c in range(3):
        x = [solved[8 * c + v] for v in range(SLICES)]
        sides = []
        for m in range(4):
            lt, rt = rx_left[4 * c + m], rx_right[4 * c + m]
            sides.append(jnp.where(side_ok, jnp.where(low, lt, roll_rows(rt, 4)), 0.0))
            sides.append(jnp.where(side_ok, jnp.where(low, roll_rows(lt, 4), rt), 0.0))
        lt, rt = rx_left[12], rx_right[12]
        under = jnp.where(low, roll_rows(lt, -c), roll_rows(rt, 4 - c))
        over = jnp.where(low, roll_rows(lt, -1 - c), roll_rows(rt, 3 - c))
        centre = (
            [jnp.where(pos == 0, ends[c], roll_rows(x[7], 1))]
            + x
            + [jnp.where(pos == 3, ends[3 + c], roll_rows(x[0], -1))]
        )
        sides = (
            [jnp.where(pos == 0, jnp.where(side_ok, under, 0.0), roll_rows(sides[7], 1))]
            + sides
            + [jnp.where(pos == 3, jnp.where(side_ok, over, 0.0), roll_rows(sides[0], -1))]
        )
        store_slices(image, (c,), stencil((centre, sides), visc_ext, weight))
        copies.append(pltpu.make_async_copy(image.at[c], image_out.at[c], sems.at[c]))
        copies[-1].start()
    for copy in copies:
        copy.wait()


def tiles_of(*lead):
    return jax.ShapeDtypeStruct(lead + TILE, jnp.float32)


def per_device(tiles, groups, velocity, forcing, viscosity, fibre, inertia):
    vel, force, fib = (a.reshape(3, 64, 128) for a in (velocity, forcing, fibre))
    visc, mass = viscosity.reshape(64, 128), inertia.reshape(64, 128)
    bind = functools.partial
    vmem = pl.BlockSpec(memory_space=pltpu.VMEM)
    hbm = pl.BlockSpec(memory_space=pltpu.HBM)
    block = jax.ShapeDtypeStruct((3, 64, 128), jnp.float32)

    def space(*shape):
        return pltpu.VMEM(shape, jnp.float32)

    def tiles_in(*lead):
        return space(*lead, *TILE)

    dma = pltpu.SemaphoreType.DMA
    inputs = [pltpu.with_memory_space_constraint(a, pltpu.HBM) for a in (vel, force, visc, fib, mass)]
    parts = pl.pallas_call(
        bind(solve_kernel, tiles, groups),
        out_shape=[tiles_of(n) for n in (24, 6, 28, 13, 13)],
        in_specs=[hbm] * 5,
        out_specs=[vmem] * 5,
        scratch_shapes=[
            space(3, 64, 128), space(3, 64, 128), space(64, 128), space(3, 64, 128), space(64, 128),
            tiles_in(16), tiles_in(16), tiles_in(2), tiles_in(1),
            tiles_in(16), tiles_in(16), tiles_in(2), tiles_in(5),
            tiles_in(6), tiles_in(groups, 6), tiles_in(2), tiles_in(groups, 2),
            tiles_in(13), tiles_in(13),
            dma((5,)), dma((14,)), dma((14,)),
            dma((groups - 2,)), dma((groups - 2,)), dma((groups - 1,)), dma((groups - 1,)),
            dma((2,)), dma((2,)), dma((2,)), dma((2,)),
            pltpu.SemaphoreType.REGULAR((groups - 2,)),
        ],
        compiler_params=pltpu.CompilerParams(
            collective_id=0, has_side_effects=True, vmem_limit_bytes=16 * 1024 * 1024
        ),
        name="solve",
    )(*inputs)
    update, image = pl.pallas_call(
        bind(image_kernel, tiles, groups),
        out_shape=[block, block],
        in_specs=[vmem] * 5,
        out_specs=[hbm] * 2,
        scratch_shapes=[space(3, 64, 128), space(3, 64, 128), dma((4,))],
        compiler_params=pltpu.CompilerParams(vmem_limit_bytes=16 * 1024 * 1024),
        name="image",
    )(*parts)
    return update.reshape(velocity.shape), image.reshape(velocity.shape)


def solution(mesh):
    wide, flat = P(None, "thick", "tile", None), P("thick", "tile", None)
    return jax.shard_map(
        functools.partial(per_device, mesh.shape["tile"], mesh.shape["thick"]),
        mesh=mesh,
        in_specs=(wide, wide, flat, wide, flat),
        out_specs=(wide, wide),
        check_vma=False,
    )
```

```python
import functools

import jax
import jax.numpy as jnp
from jax import lax
from jax.experimental import pallas as pl
from jax.experimental.pallas import tpu as pltpu
from jax.sharding import PartitionSpec as P

MESH = pl.DeviceIdType.MESH
SLICES = 8
SYM = ((0, 1, 2), (1, 3, 4), (2, 4, 5))
TILE = (8, 128)


def roll_rows(values, shift):
    return values if shift % 8 == 0 else pltpu.roll(values, shift % 8, 0)


def row_ids():
    return lax.broadcasted_iota(jnp.int32, TILE, 0)


def load_slices(ref, lead=()):
    def one(v):
        halves = [ref[lead + (pl.ds(2 * v + x, 4, stride=16), slice(None))] for x in (0, 1)]
        return jnp.concatenate(halves, axis=0)

    return [one(v) for v in range(SLICES)]


def store_slices(ref, lead, slices):
    for v in range(SLICES):
        for x in (0, 1):
            ref[lead + (pl.ds(2 * v + x, 4, stride=16), slice(None))] = slices[v][4 * x : 4 * x + 4]


def pack_rows(fields, pos):
    rows = row_ids() % 4
    packed = roll_rows(fields[0], -pos)
    for j in range(1, len(fields)):
        packed = jnp.where(rows == j, roll_rows(fields[j], j - pos), packed)
    return packed


def pack_side(ref, side, fields):
    low = row_ids() < 4
    for j, slices in enumerate(fields):
        for m in range(4):
            first, second = slices[2 * m], slices[2 * m + 1]
            if side == 0:
                ref[4 * j + m] = jnp.where(low, first, roll_rows(second, 4))
            else:
                ref[4 * j + m] = jnp.where(low, roll_rows(first, 4), second)


def greet(targets):
    barrier = pltpu.get_barrier_semaphore()
    count = 0
    for target, there in targets:
        if there is None:
            pl.semaphore_signal(barrier, inc=1, device_id=target, device_id_type=MESH)
            count = count + 1
        else:

            @pl.when(there)
            def _():
                pl.semaphore_signal(barrier, inc=1, device_id=target, device_id_type=MESH)

            count = count + there.astype(jnp.int32)
    return lambda: pl.semaphore_wait(barrier, count)


def remote(src, dst, send_sem, recv_sem, target):
    return pltpu.make_async_remote_copy(
        src_ref=src, dst_ref=dst, send_sem=send_sem, recv_sem=recv_sem,
        device_id=target, device_id_type=MESH,
    )


def when(there, action):
    pl.when(there)(lambda: action())


def edges(tiles, groups):
    t, k = lax.axis_index("tile"), lax.axis_index("thick")
    rows = row_ids()
    low = rows < 4
    side_ok = jnp.logical_or(
        jnp.logical_and(low, t > 0), jnp.logical_and(jnp.logical_not(low), t < tiles - 1)
    )
    return rows, low, side_ok, k > 0, k < groups - 1


def below_slice(slices, packed, j, has_below, rows):
    inside = roll_rows(slices[7], 1)
    return jnp.where(rows % 4 == 0, jnp.where(has_below, roll_rows(packed, -j), 0.0), inside)


def above_slice(slices, packed, j, has_above, rows):
    inside = roll_rows(slices[0], -1)
    return jnp.where(rows % 4 == 3, jnp.where(has_above, roll_rows(packed, 3 - j), 0.0), inside)


def extended(slices, j, rx_left, rx_right, rx_below, rx_rest, place):
    rows, low, side_ok, has_below, has_above = place
    sides = []
    for m in range(4):
        left, right = rx_left[4 * j + m], rx_right[4 * j + m]
        sides.append(jnp.where(side_ok, jnp.where(low, left, roll_rows(right, 4)), 0.0))
        sides.append(jnp.where(side_ok, jnp.where(low, roll_rows(left, 4), right), 0.0))
    centre = (
        [below_slice(slices, rx_below[0], j, has_below, rows)]
        + slices
        + [above_slice(slices, rx_rest[0], j, has_above, rows)]
    )
    below = roll_rows(jnp.where(low, rx_rest[2], rx_rest[1]), 4 - j)
    above = roll_rows(jnp.where(low, rx_rest[4], rx_rest[3]), 7 - j)
    below = jnp.where(jnp.logical_and(side_ok, has_below), below, 0.0)
    above = jnp.where(jnp.logical_and(side_ok, has_above), above, 0.0)
    sides = (
        [jnp.where(rows % 4 == 0, below, roll_rows(sides[7], 1))]
        + sides
        + [jnp.where(rows % 4 == 3, above, roll_rows(sides[0], -1))]
    )
    return centre, sides


def smooth(centre, sides):
    lanes = lax.broadcasted_iota(jnp.int32, TILE, 1)
    across = [c + 0.5 * (roll_rows(c, 4) + s) for c, s in zip(centre, sides)]
    out = []
    for v in range(SLICES):
        z = across[v + 1] + 0.5 * (across[v] + across[v + 2])
        up = jnp.where(lanes < 127, pltpu.roll(z, 127, 1), 0.0)
        down = jnp.where(lanes > 0, pltpu.roll(z, 1, 1), 0.0)
        out.append(z + 0.5 * (up + down))
    return out


def stencil(field, visc, weight):
    centre, sides = field
    visc_centre, visc_sides = visc
    flat = smooth(centre, sides)
    scaled = smooth(
        [a * b for a, b in zip(visc_centre, centre)], [a * b for a, b in zip(visc_sides, sides)]
    )
    return [
        (1.0 / 3.0) * (centre[v + 1] * weight[v] - visc_centre[v + 1] * flat[v] - scaled[v])
        for v in range(SLICES)
    ]


def stencil_weight(visc):
    flat = smooth(*visc)
    return [8.0 * visc[0][v + 1] + flat[v] for v in range(SLICES)]


def sym_inverse(d):
    a, b, c, e, f, g = d
    c00, c01, c02 = e * g - f * f, c * f - b * g, b * f - c * e
    r = 1.0 / (a * c00 + b * c01 + c * c02)
    return [r * q for q in (c00, c01, c02, a * g - c * c, b * c - a * f, a * e - b * b)]


def dot3(xs, ys):
    return xs[0] * ys[0] + xs[1] * ys[1] + xs[2] * ys[2]


def mat_vec(m, x):
    return [dot3(m[i], x) for i in range(3)]


def mat_mat(m, n):
    return [[dot3(m[i], [n[0][j], n[1][j], n[2][j]]) for j in range(3)] for i in range(3)]


def sym_product(m, n):
    return [dot3(m[i], [n[0][j], n[1][j], n[2][j]]) for i in range(3) for j in range(i, 3)]


def transposed(m):
    return [[m[j][i] for j in range(3)] for i in range(3)]


def full(d):
    return [[d[SYM[i][j]] for j in range(3)] for i in range(3)]


def eliminate(diag, to_prev, next_to):
    inv = full(sym_inverse(diag))
    pm = mat_mat(inv, to_prev)
    qm = mat_mat(inv, transposed(next_to))
    to_p = sym_product(transposed(to_prev), pm)
    return (inv, pm, qm), to_p, sym_product(next_to, qm), mat_mat(next_to, pm)


def push(done, source):
    inv, pm, qm = done
    return mat_vec(inv, source), mat_vec(transposed(pm), source), mat_vec(transposed(qm), source)


def back(done, y, x_prev, x_next):
    _, pm, qm = done
    return [y[i] + dot3(pm[i], x_prev) + dot3(qm[i], x_next) for i in range(3)]


def minus(a, b):
    return [x - y for x, y in zip(a, b)]


def plus(a, b):
    return [x + y for x, y in zip(a, b)]


def select(mask, a, b):
    return [jnp.where(mask, x, y) for x, y in zip(a, b)]


def keep(mask, a):
    return [jnp.where(mask, x, 0.0) for x in a]


def moved(a, shift):
    return [roll_rows(x, shift) for x in a]


def moved_mat(m, shift):
    return [moved(r, shift) for r in m]


def reduce_matrix(diag, link, pos):
    done4, to_p, to_n, passed = eliminate(diag, link, moved_mat(link, -1))
    base = keep(pos == 0, to_p)
    diag = minus(diag, plus(moved(to_n, 1), keep(pos == 1, moved(to_p, -1))))
    link = moved_mat(passed, 1)
    done5, to_p, to_n, passed = eliminate(diag, link, moved_mat(link, -2))
    base = plus(base, keep(pos == 0, moved(to_p, -1)))
    return done4, done5, base, minus(diag, moved(to_n, 2)), moved_mat(passed, 2)


def reduce_source(done4, done5, source, pos):
    y4, to_p, to_n = push(done4, source)
    base = keep(pos == 0, to_p)
    source = plus(source, plus(moved(to_n, 1), keep(pos == 1, moved(to_p, -1))))
    y5, to_p, to_n = push(done5, source)
    base = plus(base, keep(pos == 0, moved(to_p, -1)))
    return y4, y5, base, plus(source, moved(to_n, 2))


def expand_rows(done4, done5, y4, y5, x_base, x_last, pos):
    x_one = back(done5, y5, moved(x_base, 1), moved(x_last, -2))
    kept = select(pos == 1, x_one, x_last)
    x_even = back(done4, y4, select(pos == 0, x_base, moved(kept, 1)), moved(kept, -1))
    return select(pos % 2 == 0, x_even, kept)


ORDER = ((1, 0), (1, 2), (1, 4), (1, 6), (2, 1), (2, 5), (4, 3))


def solve_kernel(
    tiles, groups, vel_in, force_in, visc_in, fibre_in, mass_in,
    update, ends, visc_out, rx_left, rx_right,
    vel, force, visc, fibre, mass, tx_left, tx_right, tx_top, tx_bot,
    h_left, h_right, h_below, h_rest, matrix_own, matrix_all, source_own, source_all,
    ux_left, ux_right, load_sems, halo_send, halo_recv, mat_send, mat_recv, src_send, src_recv,
    upd_send, upd_recv, relay_send, relay_recv, reach_sems,
):
    t, k = lax.axis_index("tile"), lax.axis_index("thick")
    loads = [
        pltpu.make_async_copy(src, dst, load_sems.at[i])
        for i, (src, dst) in enumerate(
            ((visc_in, visc), (fibre_in, fibre), (vel_in, vel), (mass_in, mass), (force_in, force))
        )
    ]
    for load in loads:
        load.start()
    has_left, has_right, has_down, has_up = t > 0, t < tiles - 1, k > 0, k < groups - 1
    left, right = jnp.maximum(t - 1, 0), jnp.minimum(t + 1, tiles - 1)
    down, up = jnp.maximum(k - 1, 0), jnp.minimum(k + 1, groups - 1)
    both = jnp.logical_and
    half = groups // 2
    ring = [d for j in range(half, 0, -1) for d in sorted({j, groups - j})]
    peers = [(t, lax.rem(k + d, groups)) for d in ring]
    above, below = (t, lax.rem(k + 1, groups)), (t, lax.rem(k + groups - 1, groups))
    corner = tx_top.at[pl.ds(0, 1)]
    rest = [h_rest.at[pl.ds(i, 1)] for i in range(5)]
    plan = [
        ((t, up), has_up, has_down, tx_top, h_below),
        ((t, down), has_down, has_up, tx_bot, rest[0]),
        ((right, up), both(has_right, has_up), both(has_left, has_down), corner, rest[1]),
        ((left, up), both(has_left, has_up), both(has_right, has_down), corner, rest[2]),
        ((right, down), both(has_right, has_down), both(has_left, has_up), tx_bot, rest[3]),
        ((left, down), both(has_left, has_down), both(has_right, has_up), tx_bot, rest[4]),
    ]
    for j in (3, 0, 1, 2):
        part = pl.ds(4 * j, 4)
        plan.append(((left, k), has_left, has_right, tx_left.at[part], h_right.at[part]))
        plan.append(((right, k), has_right, has_left, tx_right.at[part], h_left.at[part]))
    near_here = greet([(p[0], p[1]) for p in plan[2:8]] + [(above, None), (below, None)])

    def tell(r):
        for side, target in enumerate((above, below)):
            pl.semaphore_signal(
                reach_sems.at[2 * r + side], inc=1, device_id=target, device_id_type=MESH
            )

    def told(r):
        for side in (0, 1):
            pl.semaphore_wait(reach_sems.at[2 * r + side], 1)

    halo = [
        (there, comes, remote(src, dst, halo_send.at[i], halo_recv.at[i], target))
        for i, (target, there, comes, src, dst) in enumerate(plan)
    ]
    for load in loads[:3]:
        load.wait()
    visc_c = load_slices(visc)
    fib = [load_slices(fibre, (c,)) for c in range(3)]
    v_c = [load_slices(vel, (c,)) for c in range(3)]
    fields = v_c + [visc_c]
    tx_bot[0] = pack_rows([f[0] for f in fields], 0)
    tx_top[0] = pack_rows([f[7] for f in fields], 3)
    tx_top[1] = pack_rows([f[7] for f in fib], 3)
    near_here()
    for there, _, copy in halo[:6]:
        when(there, copy.start)
    for i, j in enumerate((3, 0, 1, 2)):
        for side, ref in enumerate((tx_left, tx_right)):
            pack_side(ref.at[pl.ds(4 * j, 4)], side, [fields[j]])
            there, _, copy = halo[6 + 2 * i + side]
            when(there, copy.start)
    for r in range(half - 2):
        tell(r)
        told(r)
    tell(half - 2)
    place = edges(tiles, groups)
    rows, low, side_ok, has_below, has_above = place
    pos = rows % 4
    inner = pos < 3
    loads[3].wait()
    loads[4].wait()
    mass_c = load_slices(mass)
    for _, comes, copy in halo[:2]:
        when(comes, copy.wait_recv)
    centre = (
        [below_slice(visc_c, h_below[0], 3, has_below, rows)]
        + visc_c
        + [above_slice(visc_c, h_rest[0], 3, has_above, rows)]
    )
    fib = [[below_slice(fib[c], h_below[1], c, has_below, rows)] + fib[c] for c in range(3)]
    face = []
    for v in range(SLICES + 1):
        mu = 0.5 * (centre[v] + centre[v + 1])
        f = [fib[c][v] for c in range(3)]
        g = [mu * q for q in f]
        face.append(
            [mu + g[0] * f[0], g[0] * f[1], g[0] * f[2], mu + g[1] * f[1], g[1] * f[2], mu + g[2] * f[2]]
        )
    diag, link = [], []
    for v in range(SLICES):
        d = plus(face[v], face[v + 1])
        m = mass_c[v] * centre[v + 1]
        for i in (0, 3, 5):
            d[i] = d[i] + m
        diag.append(d)
        link.append(full(face[v]))
    top_diag = diag[7]
    joined = jnp.logical_or(pos > 0, has_below)
    link[0] = [keep(joined, r) for r in link[0]]
    done = []
    low_d = None
    for step, e in ORDER:
        n, p = e + step, e - step
        solved, to_p, to_n, passed = eliminate(diag[e], link[e], link[n])
        done.append(solved)
        diag[n], link[n] = minus(diag[n], to_n), passed
        if p >= 0:
            diag[p] = minus(diag[p], to_p)
        else:
            low_d = to_p if low_d is None else plus(low_d, to_p)
    d7 = minus(diag[7], keep(inner, moved(low_d, -1)))
    done4, done5, base_d, last_d, last_l = reduce_matrix(d7, link[7], pos)
    out = moved(plus(base_d, low_d), 3) + last_d + [e for r in last_l for e in r]
    for i in range(6):
        matrix_own[i] = pack_rows(out[4 * i : 4 * i + 4], 3)
    mat_copies = [
        remote(matrix_own, matrix_all.at[k], mat_send.at[i], mat_recv.at[i], p)
        for i, p in enumerate(peers[1:])
    ]
    passed_up = matrix_all.at[lax.rem(k + groups - half + 1, groups), pl.ds(0, 3)]
    passed_down = matrix_all.at[lax.rem(k + half - 1, groups), pl.ds(3, 3)]
    relays = [
        remote(passed_up, passed_up, relay_send.at[0], relay_recv.at[0], above),
        remote(passed_down, passed_down, relay_send.at[1], relay_recv.at[1], below),
    ]
    told(half - 2)
    for copy in mat_copies:
        copy.start()
    matrix_all[k] = matrix_own[...]

    for _, comes, copy in halo[2:8]:
        when(comes, copy.wait_recv)
    around = (h_left, h_right, h_below, h_rest, place)
    visc_ext = extended(visc_c, 3, *around)
    weight = stencil_weight(visc_ext)
    source = [[] for _ in range(SLICES)]
    for c in range(3):
        for _, comes, copy in halo[8 + 2 * c : 10 + 2 * c]:
            when(comes, copy.wait_recv)
        image = stencil(extended(v_c[c], c, *around), visc_ext, weight)
        force_c = load_slices(force, (c,))
        for v in range(SLICES):
            source[v].append(force_c[v] - image[v])
    top_source = source[7]
    ys = []
    low_s = None
    for (step, e), solved in zip(ORDER, done):
        n, p = e + step, e - step
        y, to_p, to_n = push(solved, source[e])
        ys.append(y)
        source[n] = plus(source[n], to_n)
        if p >= 0:
            source[p] = plus(source[p], to_p)
        else:
            low_s = to_p if low_s is None else plus(low_s, to_p)
    s7 = plus(source[7], keep(inner, moved(low_s, -1)))
    y4, y5, base_s, last_s = reduce_source(done4, done5, s7, pos)
    out = moved(plus(base_s, low_s), 3) + last_s
    source_own[0] = pack_rows(out[:4], 3)
    source_own[1] = pack_rows(out[4:], 3)
    src_copies = [
        remote(source_own, source_all.at[k], src_send.at[i], src_recv.at[i], p)
        for i, p in enumerate(peers)
    ]
    for copy in src_copies:
        copy.start()
    source_all[k] = source_own[...]
    for i in range(SLICES + 2):
        visc_out[i] = visc_ext[0][i]
        visc_out[SLICES + 2 + i] = visc_ext[1][i]
    for v in range(SLICES):
        visc_out[2 * SLICES + 4 + v] = weight[v]

    for copy, relay in zip(mat_copies[:2], relays):
        copy.wait_recv()
        relay.start()

    def gathered(ref, lo, hi, h):
        values = []
        for f in range(lo, hi):
            value = None
            for s in range(4):
                part = roll_rows(ref[2 * s + h, f // 4], s - f % 4)
                value = part if value is None else jnp.where(pos == s, part, value)
            values.append(value)
        return values

    def link_of(h):
        e = gathered(matrix_all, 12, 21, h)
        return [e[0:3], e[3:6], e[6:9]]

    for copy in mat_copies[2:] + relays:
        copy.wait_recv()
    d0 = minus(gathered(matrix_all, 6, 12, 0), gathered(matrix_all, 0, 6, 1))
    d1 = minus(
        gathered(matrix_all, 6, 12, 1), keep(inner, moved(gathered(matrix_all, 0, 6, 0), -1))
    )
    r_h, to_p, to_n, passed = eliminate(d0, link_of(0), link_of(1))
    d1 = minus(minus(d1, to_n), keep(inner, moved(to_p, -1)))
    r4, r5, _, end_d, _ = reduce_matrix(d1, passed, pos)
    end_inv = full(sym_inverse(end_d))
    face_inv = full(sym_inverse(face[8]))
    for copy in src_copies:
        copy.wait_recv()
    s0 = plus(gathered(source_all, 3, 6, 0), gathered(source_all, 0, 3, 1))
    s1 = plus(
        gathered(source_all, 3, 6, 1), keep(inner, moved(gathered(source_all, 0, 3, 0), -1))
    )
    z_h, to_p, to_n = push(r_h, s0)
    s1 = plus(plus(s1, to_n), keep(inner, moved(to_p, -1)))
    z4, z5, _, end_s = reduce_source(r4, r5, s1, pos)
    nothing = [jnp.zeros(TILE, jnp.float32)] * 3
    x1 = expand_rows(r4, r5, z4, z5, nothing, mat_vec(end_inv, end_s), pos)
    x0 = back(r_h, z_h, keep(pos > 0, moved(x1, 1)), x1)
    own, base = nothing, nothing
    for g in range(groups):
        x = (x0, x1)[g % 2]
        own = select(k == g, moved(x, 3 - g // 2), own)
        base = select(k == g + 1, moved(x, -(g // 2)), base)
    x = [None] * SLICES
    x[7] = expand_rows(done4, done5, y4, y5, base, own, pos)
    under = select(pos == 0, base, moved(x[7], 1))
    for (step, e), solved, y in reversed(list(zip(ORDER, done, ys))):
        x[e] = back(solved, y, under if e < step else x[e - step], x[e + step])
    rhs = minus(mat_vec(full(top_diag), x[7]), mat_vec(full(face[7]), x[6]))
    over = keep(has_above, mat_vec(face_inv, minus(rhs, top_source)))
    packed_base, packed_over = pack_rows(base, 0), pack_rows(over, 3)
    ux_left[12] = jnp.where(low, packed_base, roll_rows(packed_over, 4))
    ux_right[12] = jnp.where(low, roll_rows(packed_base, 4), packed_over)
    last = []
    for c in range(3):
        part = pl.ds(4 * c, 5 if c == 2 else 4)
        ways = (
            (has_left, has_right, ux_left, rx_right, (left, k)),
            (has_right, has_left, ux_right, rx_left, (right, k)),
        )
        for side, (there, comes, src, dst, target) in enumerate(ways):
            pack_side(src.at[pl.ds(4 * c, 4)], side, [[x[v][c] for v in range(SLICES)]])
            sems = upd_send.at[2 * c + side], upd_recv.at[2 * c + side]
            copy = remote(src.at[part], dst.at[part], *sems, target)
            when(there, copy.start)
            last.append((there, comes, copy))
    for c in range(3):
        for v in range(SLICES):
            update[8 * c + v] = x[v][c]
        ends[c] = base[c]
        ends[3 + c] = over[c]
    for there, _, copy in halo:
        when(there, copy.wait_send)
    for copy in mat_copies + relays + src_copies:
        copy.wait_send()
    for there, comes, copy in last:
        when(comes, copy.wait_recv)
        when(there, copy.wait_send)


def image_kernel(
    tiles, groups, solved, ends, visc, rx_left, rx_right, update_out, image_out, update, image, sems
):
    for c in range(3):
        store_slices(update, (c,), [solved[8 * c + v] for v in range(SLICES)])
    copies = [pltpu.make_async_copy(update, update_out, sems.at[3])]
    copies[0].start()
    rows, low, side_ok, has_below, has_above = edges(tiles, groups)
    pos = rows % 4
    visc_ext = ([visc[i] for i in range(10)], [visc[10 + i] for i in range(10)])
    weight = [visc[20 + v] for v in range(SLICES)]
    for c in range(3):
        x = [solved[8 * c + v] for v in range(SLICES)]
        sides = []
        for m in range(4):
            lt, rt = rx_left[4 * c + m], rx_right[4 * c + m]
            sides.append(jnp.where(side_ok, jnp.where(low, lt, roll_rows(rt, 4)), 0.0))
            sides.append(jnp.where(side_ok, jnp.where(low, roll_rows(lt, 4), rt), 0.0))
        lt, rt = rx_left[12], rx_right[12]
        under = jnp.where(low, roll_rows(lt, -c), roll_rows(rt, 4 - c))
        over = jnp.where(low, roll_rows(lt, -1 - c), roll_rows(rt, 3 - c))
        centre = (
            [jnp.where(pos == 0, ends[c], roll_rows(x[7], 1))]
            + x
            + [jnp.where(pos == 3, ends[3 + c], roll_rows(x[0], -1))]
        )
        sides = (
            [jnp.where(pos == 0, jnp.where(side_ok, under, 0.0), roll_rows(sides[7], 1))]
            + sides
            + [jnp.where(pos == 3, jnp.where(side_ok, over, 0.0), roll_rows(sides[0], -1))]
        )
        store_slices(image, (c,), stencil((centre, sides), visc_ext, weight))
        copies.append(pltpu.make_async_copy(image.at[c], image_out.at[c], sems.at[c]))
        copies[-1].start()
    for copy in copies:
        copy.wait()


def tiles_of(*lead):
    return jax.ShapeDtypeStruct(lead + TILE, jnp.float32)


def per_device(tiles, groups, velocity, forcing, viscosity, fibre, inertia):
    vel, force, fib = (a.reshape(3, 64, 128) for a in (velocity, forcing, fibre))
    visc, mass = viscosity.reshape(64, 128), inertia.reshape(64, 128)
    bind = functools.partial
    vmem = pl.BlockSpec(memory_space=pltpu.VMEM)
    hbm = pl.BlockSpec(memory_space=pltpu.HBM)
    block = jax.ShapeDtypeStruct((3, 64, 128), jnp.float32)

    def space(*shape):
        return pltpu.VMEM(shape, jnp.float32)

    def tiles_in(*lead):
        return space(*lead, *TILE)

    dma = pltpu.SemaphoreType.DMA
    inputs = [pltpu.with_memory_space_constraint(a, pltpu.HBM) for a in (vel, force, visc, fib, mass)]
    parts = pl.pallas_call(
        bind(solve_kernel, tiles, groups),
        out_shape=[tiles_of(n) for n in (24, 6, 28, 13, 13)],
        in_specs=[hbm] * 5,
        out_specs=[vmem] * 5,
        scratch_shapes=[
            space(3, 64, 128), space(3, 64, 128), space(64, 128), space(3, 64, 128), space(64, 128),
            tiles_in(16), tiles_in(16), tiles_in(2), tiles_in(1),
            tiles_in(16), tiles_in(16), tiles_in(2), tiles_in(5),
            tiles_in(6), tiles_in(groups, 6), tiles_in(2), tiles_in(groups, 2),
            tiles_in(13), tiles_in(13),
            dma((5,)), dma((14,)), dma((14,)),
            dma((groups - 2,)), dma((groups - 2,)), dma((groups - 1,)), dma((groups - 1,)),
            dma((6,)), dma((6,)), dma((2,)), dma((2,)),
            pltpu.SemaphoreType.REGULAR((groups - 2,)),
        ],
        compiler_params=pltpu.CompilerParams(
            collective_id=0, has_side_effects=True, vmem_limit_bytes=16 * 1024 * 1024
        ),
        name="solve",
    )(*inputs)
    update, image = pl.pallas_call(
        bind(image_kernel, tiles, groups),
        out_shape=[block, block],
        in_specs=[vmem] * 5,
        out_specs=[hbm] * 2,
        scratch_shapes=[space(3, 64, 128), space(3, 64, 128), dma((4,))],
        compiler_params=pltpu.CompilerParams(vmem_limit_bytes=16 * 1024 * 1024),
        name="image",
    )(*parts)
    return update.reshape(velocity.shape), image.reshape(velocity.shape)


def solution(mesh):
    wide, flat = P(None, "thick", "tile", None), P("thick", "tile", None)
    return jax.shard_map(
        functools.partial(per_device, mesh.shape["tile"], mesh.shape["thick"]),
        mesh=mesh,
        in_specs=(wide, wide, flat, wide, flat),
        out_specs=(wide, wide),
        check_vma=False,
    )
```
